32 devices in a mesh: jobs: 2 (over x), seq: 16 (over z, y, core).
Axes of the slice: x: 2, y: 2, z: 4, core: 2. Of those that a mesh axis runs over, the one named last changes fastest.
Arguments:
- queries: bfloat16 [1024, 4096], P(('jobs', 'seq')), parts along dimension 0, may hold values from -12 to 12
- keys: bfloat16 [1024, 4096], P(('jobs', 'seq')), parts along dimension 0, may hold values from -6 to 6
- values: bfloat16 [1024, 4096], P(('jobs', 'seq')), parts along dimension 0, may hold values from -6 to 6
- live_counts: int32 [2, 16], P('jobs', 'seq'), parts along dimension 0, may hold values from 4 to 16, as said below
- merge_dest: int32 [2, 1024], P('jobs', 'seq'), parts along dimension 0, may hold values from 0 to 15, as said below
- latents: float32 [2, 1024, 64], P('jobs', 'seq'), parts along dimension 0, may hold values from -6 to 6
- guidance: float32 [2], P('jobs'), parts along dimension 0, may hold values from 3 to 6
- step_index: int32 [2], P('jobs'), parts along dimension 0, may hold values from 0 to 980
- out_weight: bfloat16 [4096, 64], replicated, may hold values from -0.09375 to 0.09375
Outputs:
- denoised: float32 [2, 1024, 64], P('jobs', 'seq'), parts along dimension 0
- merged_next: float32 [2, 256, 64], P('jobs', 'seq'), parts along dimension 0
The draws below stay inside these ranges and needn't reach their ends.
There are 2 independent parts, one for each index of `jobs`. The reference program is written for one: setup_inputs(seed, part) draws one part's arguments, and reference() takes and returns one part's arrays. A program takes and returns all parts, laid end to end along the dimension named above; an argument that names none is the same for every part. Nothing has to cross between parts.
Inputs may be any that keep to these rules, and one draw needn't show every extreme that they name: `live_counts`: in every video some merge group has exactly 16 live slots. `merge_dest`: each token names a slot of its own merge group below that group's live count, and every live slot is named by at least one token.
All inputs are finite; a program needn't handle non-finite values.
Results may differ from the reference program's by a relative error of at most 0.0031.
Values may be sent and summed in bfloat16 or wider, within the bound.
No kernel may reach another device: no remote copies, remote signals or barrier semaphores. Data moves between devices by JAX's collectives and lax.ppermute only.
A program may use at most 64 MiB of HBM per device.

```python
import math
import jax
import jax.numpy as jnp
from jax import lax

HEADS = 32
HD = 128
C = 64
HALF = 64
CAP_H = 16
TIMESTEPS = 1000
STRIDE = 20
VIDEOS = 1
WIDTH = 4096
SLOTS = 256
S_TOK = 1024
N_SEQ = 16


def draw_queries(key, part):
    row_total = 2 * N_SEQ * CAP_H
    col_total = VIDEOS * HEADS * HD
    base = jnp.clip(2.0 * jax.random.normal(jax.random.fold_in(key, 1), (row_total, col_total), jnp.float32), -12.0, 12.0)
    return base.astype(jnp.bfloat16)


def draw_keys(key, part):
    row_total = 2 * N_SEQ * CAP_H
    col_total = VIDEOS * HEADS * HD
    base = jnp.clip(jax.random.normal(jax.random.fold_in(key, 2), (row_total, col_total), jnp.float32), -6.0, 6.0)
    return base.astype(jnp.bfloat16)


def merge_plan(key):
    low_count = max(2, CAP_H // 4)
    counts = jax.random.randint(jax.random.fold_in(key, 21), (VIDEOS, N_SEQ), low_count, CAP_H + 1)
    full_group = jax.random.randint(jax.random.fold_in(key, 22), (VIDEOS, 1), 0, N_SEQ)
    counts = jnp.where(jnp.arange(N_SEQ, dtype=jnp.int32)[None, :] == full_group, CAP_H, counts).astype(jnp.int32)
    scores = jax.random.randint(jax.random.fold_in(key, 23), (VIDEOS, N_SEQ, HALF), 0, 2 ** 20) * HALF + jnp.arange(HALF, dtype=jnp.int32)
    order = jnp.argsort(scores, axis=-1)
    ranks = jnp.argsort(order, axis=-1).astype(jnp.int32)
    extra = jax.random.randint(jax.random.fold_in(key, 24), (VIDEOS, N_SEQ, HALF), 0, counts[..., None])
    dest = jnp.where(ranks < counts[..., None], ranks, extra).astype(jnp.int32)
    return (counts, dest.reshape(VIDEOS, N_SEQ * HALF))


def draw_live_counts(key, part):
    counts, dest = merge_plan(key)
    return counts


def draw_merge_dest(key, part):
    counts, dest = merge_plan(key)
    return dest


def block_levels(key, shape, cuts, least, largest):
    loudness, own = 1.0, jax.random.fold_in(key, 6)
    for position, shards_of in cuts:
        draws = jnp.exp(jax.random.uniform(jax.random.fold_in(own, position), (shards_of,), jnp.float32, least / len(cuts), largest / len(cuts)))
        loudness = loudness * jnp.repeat(draws, shape[position] // shards_of).reshape([-1 if axis == position else 1 for axis in range(len(shape))])
    return loudness


def bell_draw(own_key, extent, deviation, most, split=(), held_as=jnp.bfloat16):
    entries = deviation * jax.random.normal(own_key, extent, jnp.float32)
    if split:
        entries = entries * block_levels(own_key, extent, split, -0.22, 0.18)
    return jnp.clip(entries, -most, most).astype(held_as)


def setup_inputs(seed: int = 0, part: int = 0) -> dict:
    streams_of = jax.random.split(jax.random.key(seed), 10)
    part_keys = jax.random.split(jax.random.fold_in(streams_of[9], part), 10)
    return {
        "queries": draw_queries(jax.random.fold_in(jax.random.fold_in(streams_of[9], part), 71), part),
        "keys": draw_keys(jax.random.fold_in(jax.random.fold_in(streams_of[9], part), 71), part),
        "values": bell_draw(part_keys[2], (2 * SLOTS, VIDEOS * WIDTH), 1.0, 6.0, ((0, 16),)),
        "live_counts": draw_live_counts(jax.random.fold_in(jax.random.fold_in(streams_of[9], part), 71), part),
        "merge_dest": draw_merge_dest(jax.random.fold_in(jax.random.fold_in(streams_of[9], part), 71), part),
        "latents": bell_draw(part_keys[5], (VIDEOS, S_TOK, C), 1.0, 6.0, ((1, 16),), jnp.float32),
        "guidance": jnp.clip(jax.random.uniform(part_keys[6], (VIDEOS,), jnp.float32, 3.0, 6.0), 3.0, 6.0),
        "step_index": jax.random.randint(part_keys[7], (VIDEOS,), 0, TIMESTEPS - STRIDE + 1).astype(jnp.int32),
        "out_weight": bell_draw(streams_of[8], (WIDTH, C), WIDTH ** -0.5, 0.09375),
    }


neg_big = -1e+30
shift_value = 5.0

def sigma_of(step_value):
    frac = 1.0 - step_value / TIMESTEPS
    return shift_value * frac / (1.0 + (shift_value - 1.0) * frac)

def softmax_attend(query_rows, key_rows, value_rows, key_live, score_scale):
    scores = jnp.dot(query_rows.astype(jnp.float32), key_rows.astype(jnp.float32).T, preferred_element_type=jnp.float32) * score_scale
    scores = jnp.where(key_live[None, :], scores, neg_big)
    row_top = lax.optimization_barrier(jnp.max(scores, axis=-1, keepdims=True))
    weights = jnp.exp(scores - row_top)
    probabilities = (weights / lax.optimization_barrier(jnp.sum(weights, axis=-1, keepdims=True))).astype(jnp.bfloat16)
    return jnp.dot(probabilities.astype(jnp.float32), value_rows.astype(jnp.float32), preferred_element_type=jnp.float32).astype(jnp.bfloat16)

def reference(queries, keys, values, live_counts, merge_dest, latents, guidance, step_index, out_weight):
    branch_slots = N_SEQ * CAP_H
    item_total = VIDEOS * HEADS
    score_scale = 1.0 / math.sqrt(HD)
    query_grid = queries.reshape(2, branch_slots, item_total, HD)
    key_grid = keys.reshape(2, branch_slots, item_total, HD)
    value_grid = values.reshape(2, branch_slots, item_total, HD)
    count_grid = live_counts.reshape(VIDEOS, 2, N_SEQ // 2).transpose(0, 2, 1)
    live_slots = (jnp.arange(CAP_H, dtype=jnp.int32)[None, None, None, :] < count_grid[..., None]).reshape(VIDEOS, branch_slots)

    def one_item(item_index):
        video_index = item_index // HEADS
        key_live = live_slots[video_index]
        branch_outs = [softmax_attend(query_grid[branch_no, :, item_index], key_grid[branch_no, :, item_index], value_grid[branch_no, :, item_index], key_live, score_scale) for branch_no in range(2)]
        conditioned = branch_outs[0].astype(jnp.float32)
        uncond = branch_outs[1].astype(jnp.float32)
        return (uncond + guidance[video_index] * (conditioned - uncond)).astype(jnp.bfloat16)
    guided = lax.map(one_item, jnp.arange(item_total, dtype=jnp.int32))
    guided = guided.reshape(VIDEOS, HEADS, branch_slots, HD).astype(jnp.float32)
    weight_grid = out_weight.reshape(HEADS, HD, C).astype(jnp.float32)
    merged = jnp.einsum('vhsd,hdc->vsc', guided, weight_grid)
    merged = merged.reshape(VIDEOS, N_SEQ // 2, 2, CAP_H, C).transpose(0, 2, 1, 3, 4).reshape(VIDEOS, N_SEQ, CAP_H, C)
    dest_grid = merge_dest.reshape(VIDEOS, N_SEQ, HALF)
    index_grid = jnp.broadcast_to(dest_grid[..., None], (VIDEOS, N_SEQ, HALF, C)).astype(jnp.int32)
    velocity = jnp.take_along_axis(merged, index_grid, axis=2).reshape(VIDEOS, S_TOK, C)
    step_value = step_index.astype(jnp.float32)
    sigma_now = sigma_of(step_value)
    sigma_next = sigma_of(step_value + float(STRIDE))
    denoised = latents - sigma_now[:, None, None] * velocity
    advanced = latents + (sigma_next - sigma_now)[:, None, None] * velocity
    onehot = (dest_grid[..., None] == jnp.arange(CAP_H, dtype=jnp.int32)).astype(jnp.float32)
    slot_sums = jnp.einsum('vnrj,vnrc->vnjc', onehot, advanced.reshape(VIDEOS, N_SEQ, HALF, C), precision=lax.Precision.HIGHEST)
    slot_tally = lax.optimization_barrier(jnp.sum(onehot, axis=2))
    merged_next = (slot_sums / jnp.maximum(slot_tally, 1.0)[..., None]).reshape(VIDEOS, N_SEQ * CAP_H, C)
    return (denoised, merged_next)
```

```python
import functools
import math

import jax
import jax.numpy as jnp
from jax import lax
from jax.experimental import pallas as pl
from jax.experimental.pallas import tpu as pltpu
from jax.sharding import PartitionSpec as P

HEADS = 32
HD = 128
TIMESTEPS = 1000
STRIDE = 20

neg_big = -1e30
shift_value = 5.0
dead_mark = 64.0


def sigma_of(step_value):
    frac = 1.0 - step_value / TIMESTEPS
    return shift_value * frac / (1.0 + (shift_value - 1.0) * frac)


def pack_kernel(own_ref, other_ref, place_ref, query_ref, key_ref, value_ref, out_ref):
    half, triple, per_device = out_ref.shape
    rows = triple // 3
    cap_half = rows // 2
    first_branch = place_ref[0] == 0
    row = lax.broadcasted_iota(jnp.int32, (rows, HD), 0)
    marks = []
    for video in range(own_ref.shape[0]):
        own, other = own_ref[video, 0], other_ref[video, 0]
        low = jnp.where(first_branch, own, other)
        high = jnp.where(first_branch, other, own)
        end = jnp.where(row < cap_half, low, cap_half + high)
        marks.append(jnp.where(row < end, 1.0, 0.0).astype(jnp.bfloat16))
    for item in range(half * per_device // HD):
        dest, column = divmod(item * HD, per_device)
        keep = marks[item // HEADS]
        source = slice(item * HD, (item + 1) * HD)
        target = slice(column, column + HD)
        key_tile = key_ref[:, source]
        out_ref[dest, :rows, target] = query_ref[:, source]
        out_ref[dest, rows : 2 * rows, target] = key_tile * keep + dead_mark * (1.0 - keep)
        out_ref[dest, 2 * rows :, target] = value_ref[:, source]


def attend_kernel(place_ref, guidance_ref, packed_ref, weight_ref, out_ref, *, score_scale):
    half, triple, per_device = packed_ref.shape
    rows = triple // 3
    cap_half = rows // 2
    channels = weight_ref.shape[0]
    slots = half * rows
    video = place_ref[2]
    scale = guidance_ref[video]
    factor = jnp.where(place_ref[0] == 0, scale, 1.0 - scale)
    if out_ref.shape[2] > 1:
        out_ref[...] = jnp.zeros_like(out_ref)
    block = 8 if half % 8 == 0 else half
    for start in range(0, half, block):
        total = jnp.zeros((channels, block * rows), jnp.float32)
        for item in range(per_device // HD):
            span = slice(item * HD, (item + 1) * HD)
            query = packed_ref[start : start + block, :rows, span].reshape(block * rows, HD)
            key = packed_ref[:, rows : 2 * rows, span].reshape(slots, HD)
            value = packed_ref[:, 2 * rows :, span].reshape(slots, HD)
            scores = (
                lax.dot_general(
                    key, query, (((1,), (1,)), ((), ())), preferred_element_type=jnp.float32
                )
                * score_scale
            )
            dead = key[:, :1].astype(jnp.float32) > 0.5 * dead_mark
            scores = jnp.where(dead, neg_big, scores)
            weights = jnp.exp(scores - jnp.max(scores, axis=0, keepdims=True))
            probabilities = (weights / jnp.sum(weights, axis=0, keepdims=True)).astype(jnp.bfloat16)
            attended = lax.dot_general(
                value, probabilities, (((0,), (0,)), ((), ())), preferred_element_type=jnp.float32
            ).astype(jnp.bfloat16)
            total += jnp.dot(weight_ref[:, span], attended, preferred_element_type=jnp.float32)
        part = (total * factor).T.reshape(block, 2, 2, cap_half // 2, channels)
        part = jnp.concatenate([part[:, :, 0], part[:, :, 1]], axis=-1)
        for group in range(2):
            out_ref[group, start : start + block, video] = part[:, group]


def finish_kernel(step_ref, parts_ref, dest_ref, latents_ref, denoised_ref, merged_ref):
    videos, tokens = dest_ref.shape
    channels = latents_ref.shape[2]
    cap_half = merged_ref.shape[1]
    for video in range(videos):
        lanes = jnp.sum(parts_ref[:, video], axis=0)
        merged = jnp.concatenate([lanes[:, :channels], lanes[:, channels:]], axis=0)
        slot = lax.broadcasted_iota(jnp.int32, (cap_half, tokens), 0)
        onehot = (dest_ref[video : video + 1, :] == slot).astype(jnp.float32)
        tally = jnp.sum(onehot, axis=1, keepdims=True)
        latents = latents_ref[video]
        latent_sums = jnp.dot(
            onehot, latents, precision=lax.Precision.HIGHEST, preferred_element_type=jnp.float32
        )
        velocity = lax.dot_general(
            onehot,
            merged,
            (((0,), (0,)), ((), ())),
            precision=lax.Precision.HIGHEST,
            preferred_element_type=jnp.float32,
        )
        step_value = jnp.full((1, channels), step_ref[video], jnp.int32).astype(jnp.float32)
        sigma_now = sigma_of(step_value)
        sigma_next = sigma_of(step_value + float(STRIDE))
        denoised_ref[video] = latents - sigma_now * velocity
        merged_ref[video] = (latent_sums + (sigma_next - sigma_now) * (tally * merged)) / jnp.maximum(
            tally, 1.0
        )


def local(
    queries, keys, values, live_counts, merge_dest, latents, guidance, step_index, out_weight
):
    groups = lax.axis_size("seq")
    device = lax.axis_index("seq")
    half = groups // 2
    rows, columns = queries.shape
    videos = guidance.shape[0]
    width, channels = out_weight.shape
    per_device = columns // half
    cap_half = rows // 2
    tokens = merge_dest.shape[1]
    seat = device % half
    place = jnp.stack(
        [device // half, (seat * per_device % width) // per_device, seat * per_device // width]
    ).astype(jnp.int32)
    smem = pl.BlockSpec(memory_space=pltpu.SMEM)
    vmem = pl.BlockSpec(memory_space=pltpu.VMEM)

    other_counts = lax.ppermute(live_counts, "seq", [(i, (i + half) % groups) for i in range(groups)])
    packed = pl.pallas_call(
        pack_kernel,
        out_shape=jax.ShapeDtypeStruct((half, 3 * rows, per_device), queries.dtype),
        in_specs=[smem, smem, smem, vmem, vmem, vmem],
        out_specs=vmem,
        name="pack",
    )(live_counts, other_counts, place, queries, keys, values)
    branches = [list(range(half)), list(range(half, groups))]
    gathered = lax.all_to_all(packed, "seq", 0, 0, axis_index_groups=branches, tiled=True)
    parts = pl.pallas_call(
        functools.partial(attend_kernel, score_scale=1.0 / math.sqrt(HD)),
        out_shape=jax.ShapeDtypeStruct(
            (2, half, videos, cap_half // 2, 2 * channels), jnp.float32
        ),
        grid_spec=pltpu.PrefetchScalarGridSpec(
            num_scalar_prefetch=1,
            grid=(1,),
            in_specs=[
                pl.BlockSpec(memory_space=pltpu.SMEM),
                pl.BlockSpec((half, 3 * rows, per_device), lambda i, place: (0, 0, 0)),
                pl.BlockSpec((channels, per_device), lambda i, place: (0, place[1])),
            ],
            out_specs=pl.BlockSpec(
                (2, half, videos, cap_half // 2, 2 * channels), lambda i, place: (0, 0, 0, 0, 0)
            ),
        ),
        name="attend",
    )(place, guidance, gathered, out_weight.T)
    parts = parts.reshape(groups, videos, cap_half // 2, 2 * channels)
    parts = lax.all_to_all(parts, "seq", 0, 0, tiled=True)
    return pl.pallas_call(
        finish_kernel,
        out_shape=(
            jax.ShapeDtypeStruct((videos, tokens, channels), jnp.float32),
            jax.ShapeDtypeStruct((videos, cap_half, channels), jnp.float32),
        ),
        in_specs=[smem, vmem, vmem, vmem],
        out_specs=(vmem, vmem),
        name="finish",
    )(step_index, parts, merge_dest, latents)


def solution(mesh):
    placed = (
        P(("jobs", "seq"), None),
        P(("jobs", "seq"), None),
        P(("jobs", "seq"), None),
        P("jobs", "seq"),
        P("jobs", "seq"),
        P("jobs", "seq", None),
        P("jobs"),
        P("jobs"),
        P(),
    )
    return jax.shard_map(
        local,
        mesh=mesh,
        in_specs=placed,
        out_specs=(P("jobs", "seq", None), P("jobs", "seq", None)),
        check_vma=False,
    )
```

```python
import functools
import math

import jax
import jax.numpy as jnp
from jax import lax
from jax.experimental import pallas as pl
from jax.experimental.pallas import tpu as pltpu
from jax.sharding import PartitionSpec as P

HEADS = 32
HD = 128
TIMESTEPS = 1000
STRIDE = 20

neg_big = -1e30
shift_value = 5.0
small = pltpu.CompilerParams(vmem_limit_bytes=16 * 2**20)
large = pltpu.CompilerParams(vmem_limit_bytes=32 * 2**20)
def sigma_of(step_value):
    frac = 1.0 - step_value / TIMESTEPS
    return shift_value * frac / (1.0 + (shift_value - 1.0) * frac)


def pack_kernel(query_ref, key_ref, value_ref, out_ref, sems):
    half, triple, per_device = out_ref.shape
    rows = triple // 3
    copies = []
    for part, source in enumerate((query_ref, key_ref, value_ref)):
        for dest in range(half):
            copy = pltpu.make_async_copy(
                source.at[:, pl.ds(dest * per_device, per_device)],
                out_ref.at[dest, pl.ds(part * rows, rows), :],
                sems.at[part, dest],
            )
            copy.start()
            copies.append(copy)
    for copy in copies:
        copy.wait()


def attend_kernel(
    device_ref, guidance_ref, counts_ref, packed_ref, weight_ref, out_ref, *, score_scale
):
    half, triple, per_device = packed_ref.shape
    rows = triple // 3
    cap_half = rows // 2
    channels, width = weight_ref.shape
    slots = half * rows
    device = device_ref[0]
    seat = lax.rem(device, half)
    video = seat * per_device // width
    scale = guidance_ref[video]
    factor = jnp.where(device < half, scale, 1.0 - scale)
    slot = lax.broadcasted_iota(jnp.int32, (cap_half, 1), 0)
    mask = jnp.concatenate(
        [
            jnp.where(slot < counts_ref[video, group * half + pair], 0.0, neg_big)
            for pair in range(half)
            for group in range(2)
        ],
        axis=0,
    )
    weight = weight_ref[:, pl.ds(pl.multiple_of(lax.rem(seat * per_device, width), HD), per_device)]
    if out_ref.shape[2] > 1:
        out_ref[...] = jnp.zeros_like(out_ref)
    block = 8 if half % 8 == 0 else half
    for start in range(0, half, block):
        attended = []
        for item in range(per_device // HD):
            span = slice(item * HD, (item + 1) * HD)
            query = packed_ref[start : start + block, :rows, span].reshape(block * rows, HD)
            key = packed_ref[:, rows : 2 * rows, span].reshape(slots, HD)
            value = packed_ref[:, 2 * rows :, span].reshape(slots, HD)
            scores = (
                lax.dot_general(
                    key, query, (((1,), (1,)), ((), ())), preferred_element_type=jnp.float32
                )
                * score_scale
            )
            scores = scores + mask
            weights = jnp.exp(scores - jnp.max(scores, axis=0, keepdims=True))
            probabilities = (weights / jnp.sum(weights, axis=0, keepdims=True)).astype(jnp.bfloat16)
            attended.append(
                lax.dot_general(
                    value,
                    probabilities,
                    (((0,), (0,)), ((), ())),
                    preferred_element_type=jnp.float32,
                ).astype(jnp.bfloat16)
            )
        total = jnp.dot(
            weight, jnp.concatenate(attended, axis=0), preferred_element_type=jnp.float32
        )
        part = (total * factor).T.reshape(block, 2, 2, cap_half // 2, channels)
        part = jnp.concatenate([part[:, :, 0], part[:, :, 1]], axis=-1)
        for group in range(2):
            out_ref[group, start : start + block, video] = part[:, group]


def prepare_kernel(
    step_ref, dest_ref, latents_ref, spread_ref, means_ref, gains_ref, sigma_ref
):
    videos, tokens = dest_ref.shape
    channels = latents_ref.shape[2]
    cap_half = means_ref.shape[1]
    for video in range(videos):
        slot = lax.broadcasted_iota(jnp.int32, (cap_half, tokens), 0)
        onehot = (dest_ref[video : video + 1, :] == slot).astype(jnp.float32)
        tally = jnp.sum(onehot, axis=1, keepdims=True)
        count = jnp.maximum(tally, 1.0)
        latent_sums = jnp.dot(
            onehot,
            latents_ref[video],
            precision=lax.Precision.HIGHEST,
            preferred_element_type=jnp.float32,
        )
        step_value = jnp.full((1, channels), step_ref[video], jnp.int32).astype(jnp.float32)
        sigma_now = sigma_of(step_value)
        sigma_next = sigma_of(step_value + float(STRIDE))
        spread_ref[video] = jnp.concatenate([onehot] * 3, axis=0).T.astype(jnp.bfloat16)
        means_ref[video] = latent_sums / count
        gains_ref[video] = (sigma_next - sigma_now) * (tally / count)
        sigma_ref[video] = jnp.broadcast_to(sigma_now, sigma_ref.shape[1:])


def finish_kernel(
    parts_ref, spread_ref, means_ref, gains_ref, sigma_ref, latents_ref, denoised_ref, merged_ref
):
    videos, _, channels = latents_ref.shape
    for video in range(videos):
        lanes = jnp.sum(parts_ref[:, video], axis=0)
        merged = jnp.concatenate([lanes[:, :channels], lanes[:, channels:]], axis=0)
        merged_ref[video] = means_ref[video] + gains_ref[video] * merged
        top = merged.astype(jnp.bfloat16)
        rest = merged - top.astype(jnp.float32)
        middle = rest.astype(jnp.bfloat16)
        bottom = (rest - middle.astype(jnp.float32)).astype(jnp.bfloat16)
        velocity = jnp.dot(
            spread_ref[video],
            jnp.concatenate([top, middle, bottom], axis=0),
            preferred_element_type=jnp.float32,
        )
        denoised_ref[video] = latents_ref[video] - sigma_ref[video, :1] * velocity


def local(
    queries, keys, values, live_counts, merge_dest, latents, guidance, step_index, out_weight
):
    groups = lax.axis_size("seq")
    device = lax.axis_index("seq")
    half = groups // 2
    rows, columns = queries.shape
    videos = guidance.shape[0]
    channels = out_weight.shape[1]
    per_device = columns // half
    cap_half = rows // 2
    tokens = merge_dest.shape[1]
    smem = pl.BlockSpec(memory_space=pltpu.SMEM)
    vmem = pl.BlockSpec(memory_space=pltpu.VMEM)
    hbm = pl.BlockSpec(memory_space=pl.ANY)
    f32 = jnp.float32

    packed = pl.pallas_call(
        pack_kernel,
        out_shape=jax.ShapeDtypeStruct((half, 3 * rows, per_device), queries.dtype),
        in_specs=[hbm, hbm, hbm],
        out_specs=hbm,
        scratch_shapes=[pltpu.SemaphoreType.DMA((3, half))],
        compiler_params=small,
        name="pack",
    )(*(pltpu.with_memory_space_constraint(part, pltpu.HBM) for part in (queries, keys, values)))
    branches = [list(range(half)), list(range(half, groups))]
    gathered = lax.all_to_all(packed, "seq", 0, 0, axis_index_groups=branches, tiled=True)
    seats = lax.broadcasted_iota(jnp.int32, (videos, groups), 1)
    counts = lax.psum(jnp.where(seats == device, live_counts, 0), "seq")
    parts = pl.pallas_call(
        functools.partial(attend_kernel, score_scale=1.0 / math.sqrt(HD)),
        out_shape=jax.ShapeDtypeStruct((2, half, videos, cap_half // 2, 2 * channels), f32),
        in_specs=[smem, smem, smem, vmem, vmem],
        out_specs=vmem,
        compiler_params=large,
        name="attend",
    )(device.reshape(1), guidance, counts, gathered, out_weight.T)
    parts = parts.reshape(groups, videos, cap_half // 2, 2 * channels)
    parts = lax.all_to_all(parts, "seq", 0, 0, tiled=True)
    prepared = pl.pallas_call(
        prepare_kernel,
        out_shape=(
            jax.ShapeDtypeStruct((videos, tokens, 3 * cap_half), jnp.bfloat16),
            jax.ShapeDtypeStruct((videos, cap_half, channels), f32),
            jax.ShapeDtypeStruct((videos, cap_half, channels), f32),
            jax.ShapeDtypeStruct((videos, 8, channels), f32),
        ),
        in_specs=[smem, vmem, vmem],
        out_specs=(vmem, vmem, vmem, vmem),
        compiler_params=small,
        name="prepare",
    )(step_index, merge_dest, latents)
    return pl.pallas_call(
        finish_kernel,
        out_shape=(
            jax.ShapeDtypeStruct((videos, tokens, channels), f32),
            jax.ShapeDtypeStruct((videos, cap_half, channels), f32),
        ),
        in_specs=[vmem] * 6,
        out_specs=(vmem, vmem),
        compiler_params=small,
        name="finish",
    )(parts, *prepared, latents)


def solution(mesh):
    placed = (
        P(("jobs", "seq"), None),
        P(("jobs", "seq"), None),
        P(("jobs", "seq"), None),
        P("jobs", "seq"),
        P("jobs", "seq"),
        P("jobs", "seq", None),
        P("jobs"),
        P("jobs"),
        P(),
    )
    return jax.shard_map(
        local,
        mesh=mesh,
        in_specs=placed,
        out_specs=(P("jobs", "seq", None), P("jobs", "seq", None)),
        check_vma=False,
    )
```

```python
import functools
import math

import jax
import jax.numpy as jnp
from jax import lax
from jax.experimental import pallas as pl
from jax.experimental.pallas import tpu as pltpu
from jax.sharding import PartitionSpec as P


HEADS = 32
HD = 128
TIMESTEPS = 1000
STRIDE = 20

neg_big = -1e30
shift_value = 5.0
dead_mark = 64.0
small = pltpu.CompilerParams(vmem_limit_bytes=16 * 2**20)
large = pltpu.CompilerParams(vmem_limit_bytes=32 * 2**20)
def sigma_of(step_value):
    frac = 1.0 - step_value / TIMESTEPS
    return shift_value * frac / (1.0 + (shift_value - 1.0) * frac)


def pack_kernel(device_ref, query_ref, key_ref, value_ref, *refs):
    *out_refs, sems = refs
    half = len(out_refs)
    rows, columns = query_ref.shape
    per_device = columns // half
    seat = lax.rem(device_ref[0], half)
    copies = []
    for step, out_ref in enumerate(out_refs):
        start = pl.multiple_of((seat ^ step) * per_device, HD)
        for part, source in enumerate((query_ref, key_ref, value_ref)):
            copy = pltpu.make_async_copy(
                source.at[:, pl.ds(start, per_device)],
                out_ref.at[pl.ds(part * rows, rows), :],
                sems.at[step, part],
            )
            copy.start()
            copies.append(copy)
    for copy in copies:
        copy.wait()


def mark_kernel(device_ref, own_ref, other_ref, *refs):
    half = len(refs) // 2
    triple, per_device = refs[0].shape
    rows = triple // 3
    cap_half = rows // 2
    videos = own_ref.shape[0]
    device = device_ref[0]
    seat = lax.rem(device, half)
    row = lax.broadcasted_iota(jnp.int32, (rows, HD), 0)
    for step in range(half):
        video = (seat ^ step) * videos // half
        own, other = own_ref[video, 0], other_ref[video, 0]
        low = jnp.where(device < half, own, other)
        high = jnp.where(device < half, other, own)
        end = jnp.where(row < cap_half, low, cap_half + high)
        keep = jnp.where(row < end, 1.0, 0.0).astype(jnp.bfloat16)
        mark = dead_mark * (1.0 - keep)
        for column in range(0, per_device, HD):
            place = (slice(rows, 2 * rows), slice(column, column + HD))
            refs[half + step][place] = refs[step][place] * keep + mark


def attend_kernel(
    device_ref, guidance_ref, weight_ref, *refs, score_scale
):
    *pack_refs, out_ref = refs
    half = len(pack_refs)
    triple, per_device = pack_refs[0].shape
    rows = triple // 3
    cap_half = rows // 2
    channels, width = weight_ref.shape
    device = device_ref[0]
    seat = lax.rem(device, half)
    video = seat * per_device // width
    scale = guidance_ref[video]
    factor = jnp.where(device < half, scale, 1.0 - scale)
    weight = weight_ref[:, pl.ds(pl.multiple_of(lax.rem(seat * per_device, width), HD), per_device)]
    if out_ref.shape[2] > 1:
        out_ref[...] = jnp.zeros_like(out_ref)
    block = min(half, 8)
    for first in range(0, half, block):
        attended = []
        for item in range(per_device // HD):
            span = slice(item * HD, (item + 1) * HD)
            query, key, value = (
                jnp.concatenate([ref[part * rows : (part + 1) * rows, span] for ref in chosen])
                for part, chosen in enumerate(
                    (pack_refs[first : first + block], pack_refs, pack_refs)
                )
            )
            scores = (
                lax.dot_general(
                    key, query, (((1,), (1,)), ((), ())), preferred_element_type=jnp.float32
                )
                * score_scale
            )
            dead = key[:, :1].astype(jnp.float32) > 0.5 * dead_mark
            scores = jnp.where(dead, neg_big, scores)
            weights = jnp.exp(scores - jnp.max(scores, axis=0, keepdims=True))
            probabilities = (weights / jnp.sum(weights, axis=0, keepdims=True)).astype(jnp.bfloat16)
            attended.append(
                lax.dot_general(
                    value,
                    probabilities,
                    (((0,), (0,)), ((), ())),
                    preferred_element_type=jnp.float32,
                ).astype(jnp.bfloat16)
            )
        total = jnp.dot(
            weight, jnp.concatenate(attended, axis=0), preferred_element_type=jnp.float32
        )
        part = (total * factor).T.reshape(block, 2, 2, cap_half // 2, channels)
        part = jnp.concatenate([part[:, :, 0], part[:, :, 1]], axis=-1)
        for step in range(first, first + block):
            for group in range(2):
                out_ref[group, seat ^ step, video] = part[step - first, group]


def prepare_kernel(
    step_ref, dest_ref, latents_ref, spread_ref, means_ref, gains_ref, sigma_ref
):
    videos, tokens = dest_ref.shape
    channels = latents_ref.shape[2]
    cap_half = means_ref.shape[1]
    for video in range(videos):
        slot = lax.broadcasted_iota(jnp.int32, (cap_half, tokens), 0)
        onehot = (dest_ref[video : video + 1, :] == slot).astype(jnp.float32)
        tally = jnp.sum(onehot, axis=1, keepdims=True)
        count = jnp.maximum(tally, 1.0)
        latent_sums = jnp.dot(
            onehot,
            latents_ref[video],
            precision=lax.Precision.HIGHEST,
            preferred_element_type=jnp.float32,
        )
        step_value = jnp.full((1, channels), step_ref[video], jnp.int32).astype(jnp.float32)
        sigma_now = sigma_of(step_value)
        sigma_next = sigma_of(step_value + float(STRIDE))
        spread_ref[video] = jnp.concatenate([onehot] * 3, axis=0).T.astype(jnp.bfloat16)
        means_ref[video] = latent_sums / count
        gains_ref[video] = (sigma_next - sigma_now) * (tally / count)
        sigma_ref[video] = jnp.broadcast_to(sigma_now, sigma_ref.shape[1:])


def finish_kernel(
    parts_ref, spread_ref, means_ref, gains_ref, sigma_ref, latents_ref, denoised_ref, merged_ref
):
    videos, _, channels = latents_ref.shape
    for video in range(videos):
        lanes = jnp.sum(parts_ref[:, video], axis=0)
        merged = jnp.concatenate([lanes[:, :channels], lanes[:, channels:]], axis=0)
        merged_ref[video] = means_ref[video] + gains_ref[video] * merged
        top = merged.astype(jnp.bfloat16)
        rest = merged - top.astype(jnp.float32)
        middle = rest.astype(jnp.bfloat16)
        bottom = (rest - middle.astype(jnp.float32)).astype(jnp.bfloat16)
        velocity = jnp.dot(
            spread_ref[video],
            jnp.concatenate([top, middle, bottom], axis=0),
            preferred_element_type=jnp.float32,
        )
        denoised_ref[video] = latents_ref[video] - sigma_ref[video, :1] * velocity


def local(
    queries, keys, values, live_counts, merge_dest, latents, guidance, step_index, out_weight
):
    groups = lax.axis_size("seq")
    device = lax.axis_index("seq")
    half = groups // 2
    rows, columns = queries.shape
    videos = guidance.shape[0]
    channels = out_weight.shape[1]
    per_device = columns // half
    cap_half = rows // 2
    tokens = merge_dest.shape[1]
    smem = pl.BlockSpec(memory_space=pltpu.SMEM)
    vmem = pl.BlockSpec(memory_space=pltpu.VMEM)
    hbm = pl.BlockSpec(memory_space=pl.ANY)
    f32 = jnp.float32

    seat = device.reshape(1)
    other_counts = lax.ppermute(
        live_counts, "seq", [(i, (i + half) % groups) for i in range(groups)]
    )
    pack = jax.ShapeDtypeStruct((3 * rows, per_device), queries.dtype)
    packed = pl.pallas_call(
        pack_kernel,
        out_shape=[pack] * half,
        in_specs=[smem, hbm, hbm, hbm],
        out_specs=[vmem] * half,
        scratch_shapes=[pltpu.SemaphoreType.DMA((half, 3))],
        compiler_params=small,
        name="pack",
    )(seat, *(pltpu.with_memory_space_constraint(part, pltpu.HBM) for part in (queries, keys, values)))
    packed = pl.pallas_call(
        mark_kernel,
        out_shape=[pack] * half,
        in_specs=[smem] * 3 + [vmem] * half,
        out_specs=[vmem] * half,
        input_output_aliases={3 + step: step for step in range(half)},
        compiler_params=small,
        name="mark",
    )(seat, live_counts, other_counts, *packed)
    gathered = [packed[0]] + [
        lax.ppermute(packed[step], "seq", [(i, i ^ step) for i in range(groups)])
        for step in range(1, half)
    ]
    parts = pl.pallas_call(
        functools.partial(attend_kernel, score_scale=1.0 / math.sqrt(HD)),
        out_shape=jax.ShapeDtypeStruct((2, half, videos, cap_half // 2, 2 * channels), f32),
        in_specs=[smem, smem] + [vmem] * (1 + half),
        out_specs=vmem,
        compiler_params=large,
        name="attend",
    )(seat, guidance, out_weight.T, *gathered)
    parts = parts.reshape(groups, videos, cap_half // 2, 2 * channels)
    parts = lax.all_to_all(parts, "seq", 0, 0, tiled=True)
    prepared = pl.pallas_call(
        prepare_kernel,
        out_shape=(
            jax.ShapeDtypeStruct((videos, tokens, 3 * cap_half), jnp.bfloat16),
            jax.ShapeDtypeStruct((videos, cap_half, channels), f32),
            jax.ShapeDtypeStruct((videos, cap_half, channels), f32),
            jax.ShapeDtypeStruct((videos, 8, channels), f32),
        ),
        in_specs=[smem, vmem, vmem],
        out_specs=(vmem, vmem, vmem, vmem),
        compiler_params=small,
        name="prepare",
    )(step_index, merge_dest, latents)
    return pl.pallas_call(
        finish_kernel,
        out_shape=(
            jax.ShapeDtypeStruct((videos, tokens, channels), f32),
            jax.ShapeDtypeStruct((videos, cap_half, channels), f32),
        ),
        in_specs=[vmem] * 6,
        out_specs=(vmem, vmem),
        compiler_params=small,
        name="finish",
    )(parts, *prepared, latents)


def solution(mesh):
    placed = (
        P(("jobs", "seq"), None),
        P(("jobs", "seq"), None),
        P(("jobs", "seq"), None),
        P("jobs", "seq"),
        P("jobs", "seq"),
        P("jobs", "seq", None),
        P("jobs"),
        P("jobs"),
        P(),
    )
    return jax.shard_map(
        local,
        mesh=mesh,
        in_specs=placed,
        out_specs=(P("jobs", "seq", None), P("jobs", "seq", None)),
        check_vma=False,
    )
```

```python
import functools
import math

import jax
import jax.numpy as jnp
from jax import lax
from jax.experimental import pallas as pl
from jax.experimental.pallas import tpu as pltpu
from jax.sharding import PartitionSpec as P


HD = 128
NOTE_ROWS = 8
TIMESTEPS = 1000
STRIDE = 20

neg_big = -1e30
shift_value = 5.0
small = pltpu.CompilerParams(vmem_limit_bytes=16 * 2**20)
large = pltpu.CompilerParams(vmem_limit_bytes=32 * 2**20)


def sigma_of(step_value):
    frac = 1.0 - step_value / TIMESTEPS
    return shift_value * frac / (1.0 + (shift_value - 1.0) * frac)


def pack_kernel(device_ref, query_ref, key_ref, value_ref, *refs, steps):
    *out_refs, sems = refs
    count = len(steps)
    rows, columns = query_ref.shape
    per_pair = columns // count
    seat = lax.rem(device_ref[0], 2 * count)
    copies = []
    for place, step in enumerate(steps):
        start = pl.multiple_of((seat ^ step) // 2 * per_pair, HD)
        targets = (
            (key_ref, out_refs[place].at[pl.ds(0, rows), :]),
            (value_ref, out_refs[place].at[pl.ds(rows, rows), :]),
            (query_ref, out_refs[count + place].at[pl.ds(0, rows), :]),
        )
        for part, (source, target) in enumerate(targets):
            copy = pltpu.make_async_copy(
                source.at[:, pl.ds(start, per_pair)], target, sems.at[part, place]
            )
            copy.start()
            copies.append(copy)
    for copy in copies:
        copy.wait()


def note_kernel(device_ref, own_ref, other_ref, mate_own_ref, mate_other_ref, *refs, steps, width):
    count = len(steps)
    query_refs, out_refs, home_ref = refs[: count - 1], refs[count - 1 : -1], refs[-1]
    per_pair = query_refs[0].shape[1]
    first = query_refs[0].shape[0] - NOTE_ROWS
    device = device_ref[0]
    seat = lax.rem(device, 2 * count)
    front = device < 2 * count
    row = lax.broadcasted_iota(jnp.int32, (NOTE_ROWS, HD), 0)
    note = None
    for place, step in enumerate(steps):
        if note is None or own_ref.shape[0] > 1:
            video = (seat ^ step) // 2 * per_pair // width
            note = jnp.zeros((NOTE_ROWS, HD), jnp.int32)
            for line, (own, other) in enumerate(
                ((own_ref, other_ref), (mate_own_ref, mate_other_ref))
            ):
                low = jnp.where(front, own[video, 0], other[video, 0])
                high = jnp.where(front, other[video, 0], own[video, 0])
                note = jnp.where(row == 2 * line, low, jnp.where(row == 2 * line + 1, high, note))
            note = note.astype(jnp.float32).astype(jnp.bfloat16)
        if place == 0:
            home_ref[...] = note
        else:
            for column in range(0, per_pair, HD):
                out_refs[place - 1][first : first + NOTE_ROWS, column : column + HD] = note


def attend_kernel(device_ref, guidance_ref, weight_ref, home_ref, *refs, score_scale, steps):
    *pack_refs, out_ref = refs
    count = len(steps)
    own_refs, mate_refs = pack_refs[:count], pack_refs[count : 2 * count]
    query_refs = pack_refs[2 * count :]
    rows, per_pair = own_refs[0].shape[0] // 2, own_refs[0].shape[1]
    cap_half = rows // 2
    channels, width = weight_ref.shape
    device = device_ref[0]
    seat = lax.rem(device, 2 * count)
    start = seat // 2 * per_pair
    video = start // width
    scale = guidance_ref[video]
    factor = jnp.where(device < 2 * count, scale, 1.0 - scale)
    weight = weight_ref[:, pl.ds(pl.multiple_of(lax.rem(start, width), HD), per_pair)]
    if out_ref.shape[2] > 1:
        out_ref[...] = jnp.zeros_like(out_ref)

    slot = lax.broadcasted_iota(jnp.int32, (cap_half, HD), 0).astype(jnp.float32)
    masks = []
    for line in range(2):
        for place in range(count):
            if place:
                note = query_refs[place][rows : rows + NOTE_ROWS, :HD]
            else:
                note = home_ref[...]
            note = note.astype(jnp.float32)
            for group in range(2):
                live = note[2 * line + group : 2 * line + group + 1, :]
                masks.append(jnp.where(slot < live, 0.0, neg_big))
    mask = jnp.concatenate(masks)
    sources = (*own_refs, *mate_refs)
    block = max(1, HD // rows)
    for first in range(0, count, block):
        places = range(first, min(count, first + block))
        attended = []
        for column in range(0, per_pair, HD):
            span = slice(column, column + HD)
            query = jnp.concatenate([query_refs[place][:rows, span] for place in places])
            key = jnp.concatenate([ref[:rows, span] for ref in sources])
            value = jnp.concatenate([ref[rows:, span] for ref in sources])
            scores = lax.dot_general(
                key, query, (((1,), (1,)), ((), ())), preferred_element_type=jnp.float32
            )
            scores = scores + mask[:, : query.shape[0]]
            top = jnp.max(scores, axis=0, keepdims=True)
            weights = jnp.exp2((scores - top) * (score_scale * math.log2(math.e)))
            share = 1.0 / jnp.sum(weights, axis=0, keepdims=True)
            probabilities = (weights * share).astype(jnp.bfloat16)
            attended.append(
                lax.dot_general(
                    value,
                    probabilities,
                    (((0,), (0,)), ((), ())),
                    preferred_element_type=jnp.float32,
                ).astype(jnp.bfloat16)
            )
        total = jnp.dot(
            weight, jnp.concatenate(attended, axis=0), preferred_element_type=jnp.float32
        )
        part = (total * factor).T.reshape(len(places), 2, 2, cap_half // 2, channels)
        part = jnp.concatenate([part[:, :, 0], part[:, :, 1]], axis=-1)
        for place in places:
            for group in range(2):
                out_ref[group, (seat ^ steps[place]) // 2, video] = part[place - first, group]


def prepare_kernel(
    step_ref, dest_ref, latents_ref, spread_ref, means_ref, gains_ref, sigma_ref
):
    videos, tokens = dest_ref.shape
    channels = latents_ref.shape[2]
    cap_half = means_ref.shape[1]
    for video in range(videos):
        slot = lax.broadcasted_iota(jnp.int32, (cap_half, tokens), 0)
        onehot = (dest_ref[video : video + 1, :] == slot).astype(jnp.float32)
        tally = jnp.sum(onehot, axis=1, keepdims=True)
        count = jnp.maximum(tally, 1.0)
        latent_sums = jnp.dot(
            onehot,
            latents_ref[video],
            precision=lax.Precision.HIGHEST,
            preferred_element_type=jnp.float32,
        )
        step_value = jnp.full((1, channels), step_ref[video], jnp.int32).astype(jnp.float32)
        sigma_now = sigma_of(step_value)
        sigma_next = sigma_of(step_value + float(STRIDE))
        spread_ref[video] = jnp.concatenate([onehot] * 3, axis=0).T.astype(jnp.bfloat16)
        means_ref[video] = latent_sums / count
        gains_ref[video] = (sigma_next - sigma_now) * (tally / count)
        sigma_ref[video] = jnp.broadcast_to(sigma_now, sigma_ref.shape[1:])


def finish_kernel(
    parts_ref, spread_ref, means_ref, gains_ref, sigma_ref, latents_ref, denoised_ref, merged_ref
):
    videos, _, channels = latents_ref.shape
    for video in range(videos):
        lanes = jnp.sum(parts_ref[:, video], axis=0)
        merged = jnp.concatenate([lanes[:, :channels], lanes[:, channels:]], axis=0)
        merged_ref[video] = means_ref[video] + gains_ref[video] * merged
        top = merged.astype(jnp.bfloat16)
        rest = merged - top.astype(jnp.float32)
        middle = rest.astype(jnp.bfloat16)
        bottom = (rest - middle.astype(jnp.float32)).astype(jnp.bfloat16)
        velocity = jnp.dot(
            spread_ref[video],
            jnp.concatenate([top, middle, bottom], axis=0),
            preferred_element_type=jnp.float32,
        )
        denoised_ref[video] = latents_ref[video] - sigma_ref[video, :1] * velocity


def steps_of(half):
    first = [step for step in (0, 6, 2, 4) if step < half]
    return (*first, *range(8, half, 2))


def run(
    queries, keys, values, live_counts, merge_dest, latents, guidance, step_index, out_weight
):
    groups = lax.axis_size("seq")
    device = lax.axis_index("seq")
    half = groups // 2
    count = half // 2
    rows, columns = queries.shape
    videos = guidance.shape[0]
    width, channels = out_weight.shape
    per_pair = columns // count
    cap_half = rows // 2
    tokens = merge_dest.shape[1]
    smem = pl.BlockSpec(memory_space=pltpu.SMEM)
    vmem = pl.BlockSpec(memory_space=pltpu.VMEM)
    hbm = pl.BlockSpec(memory_space=pl.ANY)
    f32 = jnp.float32
    bf16 = queries.dtype

    def swap(part, step):
        return lax.ppermute(part, "seq", [(i, i ^ step) for i in range(groups)])

    steps = steps_of(half)
    seat = device.reshape(1)
    other_counts = swap(live_counts, half)
    kv_shape = jax.ShapeDtypeStruct((2 * rows, per_pair), bf16)
    note_shape = jax.ShapeDtypeStruct((rows + NOTE_ROWS, per_pair), bf16)
    query_shapes = [jax.ShapeDtypeStruct((rows, per_pair), bf16)] + [note_shape] * (count - 1)
    packed = pl.pallas_call(
        functools.partial(pack_kernel, steps=steps),
        out_shape=[kv_shape] * count + query_shapes,
        in_specs=[smem, hbm, hbm, hbm],
        out_specs=[vmem] * (2 * count),
        scratch_shapes=[pltpu.SemaphoreType.DMA((3, count))],
        compiler_params=small,
        name="pack",
    )(seat, *(pltpu.with_memory_space_constraint(part, pltpu.HBM) for part in (queries, keys, values)))
    own, asked = packed[:count], packed[count:]
    held = [own[0]] + [swap(own[place], steps[place]) for place in range(1, count)]
    mate_own = swap(live_counts, 1)
    mate_other = swap(other_counts, 1)
    *noted, home = pl.pallas_call(
        functools.partial(note_kernel, steps=steps, width=width),
        out_shape=[note_shape] * (count - 1) + [jax.ShapeDtypeStruct((NOTE_ROWS, HD), bf16)],
        in_specs=[smem] * 5 + [vmem] * (count - 1),
        out_specs=[vmem] * count,
        input_output_aliases={5 + place: place for place in range(count - 1)},
        compiler_params=small,
        name="note",
    )(seat, live_counts, other_counts, mate_own, mate_other, *asked[1:])
    asked = [asked[0]] + [swap(noted[place - 1], steps[place]) for place in range(1, count)]
    lent = [swap(held[0], 1)] + [swap(held[place], 1) for place in range(1, count)]
    parts = pl.pallas_call(
        functools.partial(attend_kernel, score_scale=1.0 / math.sqrt(HD), steps=steps),
        out_shape=jax.ShapeDtypeStruct((2, count, videos, cap_half // 2, 2 * channels), f32),
        in_specs=[smem, smem] + [vmem] * (2 + 3 * count),
        out_specs=vmem,
        compiler_params=large,
        name="attend",
    )(seat, guidance, out_weight.T, home, *held, *lent, *asked)
    parts = parts.reshape(half, videos, cap_half // 2, 2 * channels)
    parities = [list(range(parity, groups, 2)) for parity in range(2)]
    parts = lax.all_to_all(parts, "seq", 0, 0, axis_index_groups=parities, tiled=True)
    prepared = pl.pallas_call(
        prepare_kernel,
        out_shape=(
            jax.ShapeDtypeStruct((videos, tokens, 3 * cap_half), jnp.bfloat16),
            jax.ShapeDtypeStruct((videos, cap_half, channels), f32),
            jax.ShapeDtypeStruct((videos, cap_half, channels), f32),
            jax.ShapeDtypeStruct((videos, 8, channels), f32),
        ),
        in_specs=[smem, vmem, vmem],
        out_specs=(vmem, vmem, vmem, vmem),
        compiler_params=small,
        name="prepare",
    )(step_index, merge_dest, latents)
    return pl.pallas_call(
        finish_kernel,
        out_shape=(
            jax.ShapeDtypeStruct((videos, tokens, channels), f32),
            jax.ShapeDtypeStruct((videos, cap_half, channels), f32),
        ),
        in_specs=[vmem] * 6,
        out_specs=(vmem, vmem),
        compiler_params=small,
        name="finish",
    )(parts, *prepared, latents)


def solution(mesh):
    placed = (
        P(("jobs", "seq"), None),
        P(("jobs", "seq"), None),
        P(("jobs", "seq"), None),
        P("jobs", "seq"),
        P("jobs", "seq"),
        P("jobs", "seq", None),
        P("jobs"),
        P("jobs"),
        P(),
    )
    return jax.shard_map(
        run,
        mesh=mesh,
        in_specs=placed,
        out_specs=(P("jobs", "seq", None), P("jobs", "seq", None)),
        check_vma=False,
    )
```

```python
import functools
import math

import jax
import jax.numpy as jnp
from jax import lax
from jax.experimental import pallas as pl
from jax.experimental.pallas import tpu as pltpu
from jax.sharding import PartitionSpec as P


HD = 128
NOTE_ROWS = 8
TIMESTEPS = 1000
STRIDE = 20

neg_big = -1e30
shift_value = 5.0
small = pltpu.CompilerParams(vmem_limit_bytes=16 * 2**20)
large = pltpu.CompilerParams(vmem_limit_bytes=32 * 2**20)


def sigma_of(step_value):
    frac = 1.0 - step_value / TIMESTEPS
    return shift_value * frac / (1.0 + (shift_value - 1.0) * frac)


def pack_kernel(device_ref, query_ref, key_ref, value_ref, *refs, steps):
    *out_refs, sems = refs
    count = len(steps)
    rows, columns = query_ref.shape
    per_pair = columns // count
    seat = lax.rem(device_ref[0], 2 * count)
    copies = []
    for place, step in enumerate(steps):
        start = pl.multiple_of((seat ^ step) // 2 * per_pair, HD)
        targets = (
            (key_ref, out_refs[place].at[pl.ds(0, rows), :]),
            (value_ref, out_refs[place].at[pl.ds(rows, rows), :]),
            (query_ref, out_refs[count + place].at[pl.ds(0, rows), :]),
        )
        for part, (source, target) in enumerate(targets):
            copy = pltpu.make_async_copy(
                source.at[:, pl.ds(start, per_pair)], target, sems.at[part, place]
            )
            copy.start()
            copies.append(copy)
    for copy in copies:
        copy.wait()


def live_count(dest_ref, video):
    return jnp.max(dest_ref[pl.ds(video, 1), :], axis=1, keepdims=True) + 1


def note_kernel(device_ref, own_ref, other_ref, mate_dest_ref, mate_other_ref, *refs, steps, width):
    count = len(steps)
    query_refs, out_refs, home_ref = refs[: count - 1], refs[count - 1 : -1], refs[-1]
    per_pair = query_refs[0].shape[1]
    first = query_refs[0].shape[0] - NOTE_ROWS
    device = device_ref[0]
    seat = lax.rem(device, 2 * count)
    front = device < 2 * count
    row = lax.broadcasted_iota(jnp.int32, (NOTE_ROWS, HD), 0)
    note = None
    for place, step in enumerate(steps):
        if note is None or own_ref.shape[0] > 1:
            video = (seat ^ step) // 2 * per_pair // width if own_ref.shape[0] > 1 else 0
            note = jnp.zeros((NOTE_ROWS, HD), jnp.int32)
            for line, (own, other) in enumerate(
                ((own_ref, other_ref), (mate_dest_ref, mate_other_ref))
            ):
                own, other = live_count(own, video), live_count(other, video)
                low, high = jnp.where(front, own, other), jnp.where(front, other, own)
                note = jnp.where(row == 2 * line, low, jnp.where(row == 2 * line + 1, high, note))
            note = note.astype(jnp.float32).astype(jnp.bfloat16)
        if place == 0:
            home_ref[...] = note
        else:
            for column in range(0, per_pair, HD):
                out_refs[place - 1][first : first + NOTE_ROWS, column : column + HD] = note


def attend_kernel(device_ref, guidance_ref, weight_ref, home_ref, *refs, score_scale, steps):
    *pack_refs, out_ref = refs
    count = len(steps)
    own_refs, mate_refs = pack_refs[:count], pack_refs[count : 2 * count]
    query_refs = pack_refs[2 * count :]
    rows, per_pair = own_refs[0].shape[0] // 2, own_refs[0].shape[1]
    cap_half = rows // 2
    channels, width = weight_ref.shape
    device = device_ref[0]
    seat = lax.rem(device, 2 * count)
    start = seat // 2 * per_pair
    video = start // width
    scale = guidance_ref[video]
    factor = jnp.where(device < 2 * count, scale, 1.0 - scale)
    weight = weight_ref[:, pl.ds(pl.multiple_of(lax.rem(start, width), HD), per_pair)]
    if out_ref.shape[2] > 1:
        out_ref[...] = jnp.zeros_like(out_ref)

    slot = lax.broadcasted_iota(jnp.int32, (cap_half, HD), 0).astype(jnp.float32)
    masks = []
    for line in range(2):
        for place in range(count):
            if place:
                note = query_refs[place][rows : rows + NOTE_ROWS, :HD]
            else:
                note = home_ref[...]
            note = note.astype(jnp.float32)
            for group in range(2):
                live = note[2 * line + group : 2 * line + group + 1, :]
                masks.append(jnp.where(slot < live, 0.0, neg_big))
    mask = jnp.concatenate(masks)
    sources = (*own_refs, *mate_refs)
    block = max(1, HD // rows)
    for first in range(0, count, block):
        places = range(first, min(count, first + block))
        attended = []
        for column in range(0, per_pair, HD):
            span = slice(column, column + HD)
            query = jnp.concatenate([query_refs[place][:rows, span] for place in places])
            key = jnp.concatenate([ref[:rows, span] for ref in sources])
            value = jnp.concatenate([ref[rows:, span] for ref in sources])
            scores = lax.dot_general(
                key, query, (((1,), (1,)), ((), ())), preferred_element_type=jnp.float32
            )
            scores = scores + mask[:, : query.shape[0]]
            top = jnp.max(scores, axis=0, keepdims=True)
            weights = jnp.exp2((scores - top) * (score_scale * math.log2(math.e)))
            share = 1.0 / jnp.sum(weights, axis=0, keepdims=True)
            probabilities = (weights * share).astype(jnp.bfloat16)
            attended.append(
                lax.dot_general(
                    value,
                    probabilities,
                    (((0,), (0,)), ((), ())),
                    preferred_element_type=jnp.float32,
                ).astype(jnp.bfloat16)
            )
        total = jnp.dot(
            weight, jnp.concatenate(attended, axis=0), preferred_element_type=jnp.float32
        )
        part = (total * factor).T.reshape(len(places), 2, 2, cap_half // 2, channels)
        part = jnp.concatenate([part[:, :, 0], part[:, :, 1]], axis=-1)
        for place in places:
            for group in range(2):
                out_ref[group, (seat ^ steps[place]) // 2, video] = part[place - first, group]


def prepare_kernel(
    step_ref, dest_ref, latents_ref, spread_ref, means_ref, gains_ref, sigma_ref
):
    videos, tokens = dest_ref.shape
    channels = latents_ref.shape[2]
    cap_half = means_ref.shape[1]
    for video in range(videos):
        slot = lax.broadcasted_iota(jnp.int32, (cap_half, tokens), 0)
        onehot = (dest_ref[video : video + 1, :] == slot).astype(jnp.float32)
        tally = jnp.sum(onehot, axis=1, keepdims=True)
        count = jnp.maximum(tally, 1.0)
        latent_sums = jnp.dot(
            onehot,
            latents_ref[video],
            precision=lax.Precision.HIGHEST,
            preferred_element_type=jnp.float32,
        )
        step_value = jnp.full((1, channels), step_ref[video], jnp.int32).astype(jnp.float32)
        sigma_now = sigma_of(step_value)
        sigma_next = sigma_of(step_value + float(STRIDE))
        spread_ref[video] = jnp.concatenate([onehot] * 3, axis=0).T.astype(jnp.bfloat16)
        means_ref[video] = latent_sums / count
        gains_ref[video] = (sigma_next - sigma_now) * (tally / count)
        sigma_ref[video] = jnp.broadcast_to(sigma_now, sigma_ref.shape[1:])


def finish_kernel(
    parts_ref, spread_ref, means_ref, gains_ref, sigma_ref, latents_ref, denoised_ref, merged_ref
):
    videos, _, channels = latents_ref.shape
    for video in range(videos):
        lanes = jnp.sum(parts_ref[:, video], axis=0)
        merged = jnp.concatenate([lanes[:, :channels], lanes[:, channels:]], axis=0)
        merged_ref[video] = means_ref[video] + gains_ref[video] * merged
        top = merged.astype(jnp.bfloat16)
        rest = merged - top.astype(jnp.float32)
        middle = rest.astype(jnp.bfloat16)
        bottom = (rest - middle.astype(jnp.float32)).astype(jnp.bfloat16)
        velocity = jnp.dot(
            spread_ref[video],
            jnp.concatenate([top, middle, bottom], axis=0),
            preferred_element_type=jnp.float32,
        )
        denoised_ref[video] = latents_ref[video] - sigma_ref[video, :1] * velocity


def steps_of(half):
    first = [step for step in (0, 6, 2, 4) if step < half]
    return (*first, *range(8, half, 2))


def run(
    queries, keys, values, live_counts, merge_dest, latents, guidance, step_index, out_weight
):
    groups = lax.axis_size("seq")
    device = lax.axis_index("seq")
    half = groups // 2
    count = half // 2
    rows, columns = queries.shape
    videos = guidance.shape[0]
    width, channels = out_weight.shape
    per_pair = columns // count
    cap_half = rows // 2
    tokens = merge_dest.shape[1]
    smem = pl.BlockSpec(memory_space=pltpu.SMEM)
    vmem = pl.BlockSpec(memory_space=pltpu.VMEM)
    hbm = pl.BlockSpec(memory_space=pl.ANY)
    f32 = jnp.float32
    bf16 = queries.dtype

    def swap(part, step):
        return lax.ppermute(part, "seq", [(i, i ^ step) for i in range(groups)])

    steps = steps_of(half)
    seat = device.reshape(1)
    other_dest = swap(merge_dest, half)
    kv_shape = jax.ShapeDtypeStruct((2 * rows, per_pair), bf16)
    note_shape = jax.ShapeDtypeStruct((rows + NOTE_ROWS, per_pair), bf16)
    query_shapes = [jax.ShapeDtypeStruct((rows, per_pair), bf16)] + [note_shape] * (count - 1)
    packed = pl.pallas_call(
        functools.partial(pack_kernel, steps=steps),
        out_shape=[kv_shape] * count + query_shapes,
        in_specs=[smem, hbm, hbm, hbm],
        out_specs=[vmem] * (2 * count),
        scratch_shapes=[pltpu.SemaphoreType.DMA((3, count))],
        compiler_params=small,
        name="pack",
    )(seat, *(pltpu.with_memory_space_constraint(part, pltpu.HBM) for part in (queries, keys, values)))
    own, asked = packed[:count], packed[count:]
    held = [own[0]] + [swap(own[place], steps[place]) for place in range(1, count)]
    mate_dest = swap(merge_dest, 1)
    mate_other = swap(other_dest, 1)
    *noted, home = pl.pallas_call(
        functools.partial(note_kernel, steps=steps, width=width),
        out_shape=[note_shape] * (count - 1) + [jax.ShapeDtypeStruct((NOTE_ROWS, HD), bf16)],
        in_specs=[smem] + [vmem] * (count + 3),
        out_specs=[vmem] * count,
        input_output_aliases={5 + place: place for place in range(count - 1)},
        compiler_params=small,
        name="note",
    )(
        seat,
        *(
            pltpu.with_memory_space_constraint(part, pltpu.VMEM)
            for part in (merge_dest, other_dest, mate_dest, mate_other)
        ),
        *asked[1:],
    )
    asked = [asked[0]] + [swap(noted[place - 1], steps[place]) for place in range(1, count)]
    lent = [swap(held[0], 1)] + [swap(held[place], 1) for place in range(1, count)]
    parts = pl.pallas_call(
        functools.partial(attend_kernel, score_scale=1.0 / math.sqrt(HD), steps=steps),
        out_shape=jax.ShapeDtypeStruct((2, count, videos, cap_half // 2, 2 * channels), f32),
        in_specs=[smem, smem] + [vmem] * (2 + 3 * count),
        out_specs=vmem,
        compiler_params=large,
        name="attend",
    )(seat, guidance, out_weight.T, home, *held, *lent, *asked)
    parts = parts.reshape(half, videos, cap_half // 2, 2 * channels)
    parities = [list(range(parity, groups, 2)) for parity in range(2)]
    parts = lax.all_to_all(parts, "seq", 0, 0, axis_index_groups=parities, tiled=True)
    prepared = pl.pallas_call(
        prepare_kernel,
        out_shape=(
            jax.ShapeDtypeStruct((videos, tokens, 3 * cap_half), jnp.bfloat16),
            jax.ShapeDtypeStruct((videos, cap_half, channels), f32),
            jax.ShapeDtypeStruct((videos, cap_half, channels), f32),
            jax.ShapeDtypeStruct((videos, 8, channels), f32),
        ),
        in_specs=[smem, vmem, vmem],
        out_specs=(vmem, vmem, vmem, vmem),
        compiler_params=small,
        name="prepare",
    )(step_index, merge_dest, latents)
    return pl.pallas_call(
        finish_kernel,
        out_shape=(
            jax.ShapeDtypeStruct((videos, tokens, channels), f32),
            jax.ShapeDtypeStruct((videos, cap_half, channels), f32),
        ),
        in_specs=[vmem] * 6,
        out_specs=(vmem, vmem),
        compiler_params=small,
        name="finish",
    )(parts, *prepared, latents)


def solution(mesh):
    placed = (
        P(("jobs", "seq"), None),
        P(("jobs", "seq"), None),
        P(("jobs", "seq"), None),
        P("jobs", "seq"),
        P("jobs", "seq"),
        P("jobs", "seq", None),
        P("jobs"),
        P("jobs"),
        P(),
    )
    return jax.shard_map(
        run,
        mesh=mesh,
        in_specs=placed,
        out_specs=(P("jobs", "seq", None), P("jobs", "seq", None)),
        check_vma=False,
    )
```

```python
import functools
import math

import jax
import jax.numpy as jnp
from jax import lax
from jax.experimental import pallas as pl
from jax.experimental.pallas import tpu as pltpu
from jax.sharding import PartitionSpec as P


HD = 128
NOTE_ROWS = 8
FOLD = 2
TIMESTEPS = 1000
STRIDE = 20

neg_big = -1e30
shift_value = 5.0
small = pltpu.CompilerParams(vmem_limit_bytes=16 * 2**20)
large = pltpu.CompilerParams(vmem_limit_bytes=32 * 2**20)


def sigma_of(step_value):
    frac = 1.0 - step_value / TIMESTEPS
    return shift_value * frac / (1.0 + (shift_value - 1.0) * frac)


def fetch(pieces, sems):
    copies = []
    for number, (source, target) in enumerate(pieces):
        copies.append(pltpu.make_async_copy(source, target, sems.at[number]))
        copies[-1].start()
    for copy in copies:
        copy.wait()


def pack_kernel(device_ref, query_ref, key_ref, value_ref, *refs, steps):
    *out_refs, sems = refs
    count = len(steps)
    rows, columns = query_ref.shape
    per_pair = columns // count
    seat = lax.rem(device_ref[0], 2 * count)
    pieces = []
    for place, step in enumerate(steps):
        start = (seat ^ step) // 2 * per_pair
        span = pl.ds(pl.multiple_of(start, HD), per_pair)
        pieces.append((key_ref.at[:, span], out_refs[place].at[pl.ds(0, rows), :]))
        pieces.append((value_ref.at[:, span], out_refs[place].at[pl.ds(rows, rows), :]))
        folded = per_pair // FOLD
        for fold in range(FOLD):
            span = pl.ds(pl.multiple_of(start + fold * folded, HD), folded)
            target = out_refs[count + place].at[pl.ds(fold * rows, rows), :]
            pieces.append((query_ref.at[:, span], target))
    fetch(pieces, sems)


def live_count(dest_ref, video):
    return jnp.max(dest_ref[pl.ds(video, 1), :], axis=1, keepdims=True) + 1


def note_kernel(device_ref, own_ref, other_ref, mate_dest_ref, mate_other_ref, *refs, steps):
    count = len(steps)
    query_refs, out_refs, home_ref = refs[: count - 1], refs[count - 1 : -1], refs[-1]
    first = query_refs[0].shape[0] - NOTE_ROWS
    device = device_ref[0]
    seat = lax.rem(device, 2 * count)
    front = device < 2 * count
    row = lax.broadcasted_iota(jnp.int32, (NOTE_ROWS, HD), 0)
    note = None
    for place, step in enumerate(steps):
        if note is None or own_ref.shape[0] > 1:
            video = (seat ^ step) // 2 * own_ref.shape[0] // count if own_ref.shape[0] > 1 else 0
            note = jnp.zeros((NOTE_ROWS, HD), jnp.int32)
            for line, (own, other) in enumerate(
                ((own_ref, other_ref), (mate_dest_ref, mate_other_ref))
            ):
                own, other = live_count(own, video), live_count(other, video)
                low, high = jnp.where(front, own, other), jnp.where(front, other, own)
                note = jnp.where(row == 2 * line, low, jnp.where(row == 2 * line + 1, high, note))
            note = note.astype(jnp.float32).astype(jnp.bfloat16)
        if place == 0:
            home_ref[...] = note
        else:
            out_refs[place - 1][first : first + NOTE_ROWS, :HD] = note


def attend_kernel(device_ref, guidance_ref, weight_ref, home_ref, *refs, score_scale, steps):
    count = len(steps)
    pack_refs, out_refs = refs[:-count], refs[-count:]
    own_refs, mate_refs = pack_refs[:count], pack_refs[count : 2 * count]
    query_refs = pack_refs[2 * count :]
    rows, per_pair = own_refs[0].shape[0] // 2, own_refs[0].shape[1]
    cap_half = rows // 2
    channels, width = weight_ref.shape
    device = device_ref[0]
    seat = lax.rem(device, 2 * count)
    start = seat // 2 * per_pair
    video = start // width
    scale = guidance_ref[video]
    front = device < 2 * count
    factor = jnp.where(front, scale, 1.0 - scale)
    weight = weight_ref[:, pl.ds(pl.multiple_of(lax.rem(start, width), HD), per_pair)]
    if out_refs[0].shape[1] > 1:
        for out_ref in out_refs:
            out_ref[...] = jnp.zeros_like(out_ref)

    slot = lax.broadcasted_iota(jnp.int32, (cap_half, HD), 0).astype(jnp.float32)
    masks = []
    for line in range(2):
        for place in range(count):
            if place:
                note = query_refs[place][FOLD * rows :, :HD]
            else:
                note = home_ref[...]
            note = note.astype(jnp.float32)
            for group in range(2):
                live = note[2 * line + group : 2 * line + group + 1, :]
                masks.append(jnp.where(slot < live, 0.0, neg_big))
    mask = jnp.concatenate(masks)
    sources = (*own_refs, *mate_refs)
    block = max(1, HD // rows)
    for first in range(0, count, block):
        places = range(first, min(count, first + block))
        attended = []
        for column in range(0, per_pair, HD):
            span = slice(column, column + HD)
            fold, lane = divmod(column, per_pair // FOLD)
            query = jnp.concatenate(
                [
                    query_refs[place][fold * rows : (fold + 1) * rows, lane : lane + HD]
                    for place in places
                ]
            )
            key = jnp.concatenate([ref[:rows, span] for ref in sources])
            value = jnp.concatenate([ref[rows:, span] for ref in sources])
            scores = lax.dot_general(
                key, query, (((1,), (1,)), ((), ())), preferred_element_type=jnp.float32
            )
            scores = scores + mask[:, : query.shape[0]]
            top = jnp.max(scores, axis=0, keepdims=True)
            weights = jnp.exp2((scores - top) * (score_scale * math.log2(math.e)))
            share = 1.0 / jnp.sum(weights, axis=0, keepdims=True)
            probabilities = (weights * share).astype(jnp.bfloat16)
            attended.append(
                lax.dot_general(
                    value,
                    probabilities,
                    (((0,), (0,)), ((), ())),
                    preferred_element_type=jnp.float32,
                ).astype(jnp.bfloat16)
            )
        total = jnp.dot(
            weight, jnp.concatenate(attended, axis=0), preferred_element_type=jnp.float32
        )
        part = (total * factor).T.reshape(len(places), 2, 2, cap_half // 2, channels)
        part = jnp.concatenate([part[:, :, 0], part[:, :, 1]], axis=-1)
        for place in places:
            near, far = part[place - first, 0], part[place - first, 1]
            near, far = jnp.where(front, near, far), jnp.where(front, far, near)
            quad, line = steps[place] // 4, steps[place] // 2 % 2
            out_refs[quad][line, video] = near
            out_refs[count // 2 + quad][line, video] = far


def gather_kernel(*refs):
    *part_refs, kept_ref, sent_ref = refs
    for line, out_ref in enumerate((kept_ref, sent_ref)):
        terms = [ref[line] for ref in part_refs]
        while len(terms) > 1:
            terms = [sum(terms[i : i + 2]) for i in range(0, len(terms), 2)]
        out_ref[...] = terms[0]


def prepare_kernel(
    step_ref, dest_ref, latents_ref, spread_ref, means_ref, gains_ref, sigma_ref
):
    videos, tokens = dest_ref.shape
    channels = latents_ref.shape[2]
    cap_half = means_ref.shape[1]
    for video in range(videos):
        slot = lax.broadcasted_iota(jnp.int32, (cap_half, tokens), 0)
        onehot = (dest_ref[video : video + 1, :] == slot).astype(jnp.float32)
        tally = jnp.sum(onehot, axis=1, keepdims=True)
        count = jnp.maximum(tally, 1.0)
        latent_sums = jnp.dot(
            onehot,
            latents_ref[video],
            precision=lax.Precision.HIGHEST,
            preferred_element_type=jnp.float32,
        )
        step_value = jnp.full((1, channels), step_ref[video], jnp.int32).astype(jnp.float32)
        sigma_now = sigma_of(step_value)
        sigma_next = sigma_of(step_value + float(STRIDE))
        spread_ref[video] = jnp.concatenate([onehot] * 3, axis=0).T.astype(jnp.bfloat16)
        means_ref[video] = latent_sums / count
        gains_ref[video] = (sigma_next - sigma_now) * (tally / count)
        sigma_ref[video] = jnp.broadcast_to(sigma_now, sigma_ref.shape[1:])


def finish_kernel(
    kept_ref,
    came_ref,
    spread_ref,
    means_ref,
    gains_ref,
    sigma_ref,
    latents_ref,
    denoised_ref,
    merged_ref,
):
    videos, _, channels = latents_ref.shape
    for video in range(videos):
        lanes = kept_ref[video] + came_ref[video]
        merged = jnp.concatenate([lanes[:, :channels], lanes[:, channels:]], axis=0)
        merged_ref[video] = means_ref[video] + gains_ref[video] * merged
        top = merged.astype(jnp.bfloat16)
        rest = merged - top.astype(jnp.float32)
        middle = rest.astype(jnp.bfloat16)
        bottom = (rest - middle.astype(jnp.float32)).astype(jnp.bfloat16)
        velocity = jnp.dot(
            spread_ref[video],
            jnp.concatenate([top, middle, bottom], axis=0),
            preferred_element_type=jnp.float32,
        )
        denoised_ref[video] = latents_ref[video] - sigma_ref[video, :1] * velocity


def steps_of(half):
    first = [step for step in (0, 6, 2, 4) if step < half]
    return (*first, *range(8, half, 2))


def run(
    queries, keys, values, live_counts, merge_dest, latents, guidance, step_index, out_weight
):
    groups = lax.axis_size("seq")
    device = lax.axis_index("seq")
    half = groups // 2
    count = half // 2
    rows, columns = queries.shape
    videos = guidance.shape[0]
    _, channels = out_weight.shape
    per_pair = columns // count
    cap_half = rows // 2
    tokens = merge_dest.shape[1]
    smem = pl.BlockSpec(memory_space=pltpu.SMEM)
    vmem = pl.BlockSpec(memory_space=pltpu.VMEM)
    hbm = pl.BlockSpec(memory_space=pl.ANY)
    f32 = jnp.float32
    bf16 = queries.dtype

    def swap(part, step):
        return lax.ppermute(part, "seq", [(i, i ^ step) for i in range(groups)])

    steps = steps_of(half)
    seat = device.reshape(1)
    other_dest = swap(merge_dest, half)
    kv_shape = jax.ShapeDtypeStruct((2 * rows, per_pair), bf16)
    note_shape = jax.ShapeDtypeStruct((FOLD * rows + NOTE_ROWS, per_pair // FOLD), bf16)
    query_shape = jax.ShapeDtypeStruct((FOLD * rows, per_pair // FOLD), bf16)
    query_shapes = [query_shape] + [note_shape] * (count - 1)
    sources = [pltpu.with_memory_space_constraint(part, pltpu.HBM) for part in (queries, keys, values)]
    packed = pl.pallas_call(
        functools.partial(pack_kernel, steps=steps),
        out_shape=[kv_shape] * count + query_shapes,
        in_specs=[smem, hbm, hbm, hbm],
        out_specs=[vmem] * (2 * count),
        scratch_shapes=[pltpu.SemaphoreType.DMA((count * (2 + FOLD),))],
        compiler_params=small,
        name="pack",
    )(seat, *sources)
    own, asked = packed[:count], packed[count:]
    held = [own[0]] + [swap(own[place], steps[place]) for place in range(1, count)]
    mate_dest = swap(merge_dest, 1)
    mate_other = swap(other_dest, 1)
    *noted, home = pl.pallas_call(
        functools.partial(note_kernel, steps=steps),
        out_shape=[note_shape] * (count - 1) + [jax.ShapeDtypeStruct((NOTE_ROWS, HD), bf16)],
        in_specs=[smem] + [vmem] * (count + 3),
        out_specs=[vmem] * count,
        input_output_aliases={5 + place: place for place in range(count - 1)},
        compiler_params=small,
        name="note",
    )(
        seat,
        *(
            pltpu.with_memory_space_constraint(part, pltpu.VMEM)
            for part in (merge_dest, other_dest, mate_dest, mate_other)
        ),
        *asked[1:],
    )
    asked = [asked[0]] + [swap(noted[place - 1], steps[place]) for place in range(1, count)]
    lent = [swap(held[0], 1)] + [swap(held[place], 1) for place in range(1, count)]
    part_shape = (videos, cap_half // 2, 2 * channels)
    parts = pl.pallas_call(
        functools.partial(attend_kernel, score_scale=1.0 / math.sqrt(HD), steps=steps),
        out_shape=[jax.ShapeDtypeStruct((2, *part_shape), f32)] * count,
        in_specs=[smem, smem] + [vmem] * (1 + 1 + 3 * count),
        out_specs=[vmem] * count,
        compiler_params=large,
        name="attend",
    )(seat, guidance, out_weight.T, home, *held, *lent, *asked)
    parts = [parts[0]] + [swap(parts[quad], 4 * quad) for quad in range(1, count)]
    kept, sent = pl.pallas_call(
        gather_kernel,
        out_shape=[jax.ShapeDtypeStruct(part_shape, f32)] * 2,
        in_specs=[vmem] * count,
        out_specs=[vmem] * 2,
        compiler_params=small,
        name="gather",
    )(*parts)
    came = swap(sent, 2)
    prepared = pl.pallas_call(
        prepare_kernel,
        out_shape=(
            jax.ShapeDtypeStruct((videos, tokens, 3 * cap_half), jnp.bfloat16),
            jax.ShapeDtypeStruct((videos, cap_half, channels), f32),
            jax.ShapeDtypeStruct((videos, cap_half, channels), f32),
            jax.ShapeDtypeStruct((videos, 8, channels), f32),
        ),
        in_specs=[smem, vmem, vmem],
        out_specs=(vmem, vmem, vmem, vmem),
        compiler_params=small,
        name="prepare",
    )(step_index, merge_dest, latents)
    return pl.pallas_call(
        finish_kernel,
        out_shape=(
            jax.ShapeDtypeStruct((videos, tokens, channels), f32),
            jax.ShapeDtypeStruct((videos, cap_half, channels), f32),
        ),
        in_specs=[vmem] * 7,
        out_specs=(vmem, vmem),
        compiler_params=small,
        name="finish",
    )(kept, came, *prepared, latents)


def solution(mesh):
    placed = (
        P(("jobs", "seq"), None),
        P(("jobs", "seq"), None),
        P(("jobs", "seq"), None),
        P("jobs", "seq"),
        P("jobs", "seq"),
        P("jobs", "seq", None),
        P("jobs"),
        P("jobs"),
        P(),
    )
    return jax.shard_map(
        run,
        mesh=mesh,
        in_specs=placed,
        out_specs=(P("jobs", "seq", None), P("jobs", "seq", None)),
        check_vma=False,
    )
```

```python
import functools
import math

import jax
import jax.numpy as jnp
from jax import lax
from jax.experimental import pallas as pl
from jax.experimental.pallas import tpu as pltpu
from jax.sharding import PartitionSpec as P


HD = 128
NOTE_ROWS = 8
FOLD = 2
TIMESTEPS = 1000
STRIDE = 20

neg_big = -1e30
shift_value = 5.0
small = pltpu.CompilerParams(vmem_limit_bytes=16 * 2**20)
large = pltpu.CompilerParams(vmem_limit_bytes=32 * 2**20)


def sigma_of(step_value):
    frac = 1.0 - step_value / TIMESTEPS
    return shift_value * frac / (1.0 + (shift_value - 1.0) * frac)


def fetch(pieces, sems):
    copies = []
    for number, (source, target) in enumerate(pieces):
        copies.append(pltpu.make_async_copy(source, target, sems.at[number]))
        copies[-1].start()
    for copy in copies:
        copy.wait()


def pack_kernel(device_ref, query_ref, key_ref, value_ref, *refs, steps):
    *out_refs, sems = refs
    count = len(steps)
    rows, columns = query_ref.shape
    per_pair = columns // count
    seat = lax.rem(device_ref[0], 2 * count)
    pieces = []
    for place, step in enumerate(steps):
        start = (seat ^ step) // 2 * per_pair
        span = pl.ds(pl.multiple_of(start, HD), per_pair)
        pieces.append((key_ref.at[:, span], out_refs[place].at[pl.ds(0, rows), :]))
        pieces.append((value_ref.at[:, span], out_refs[place].at[pl.ds(rows, rows), :]))
        folded = per_pair // FOLD
        for fold in range(FOLD):
            span = pl.ds(pl.multiple_of(start + fold * folded, HD), folded)
            target = out_refs[count + place].at[pl.ds(fold * rows, rows), :]
            pieces.append((query_ref.at[:, span], target))
    fetch(pieces, sems)


def live_count(dest_ref, video):
    return jnp.max(dest_ref[pl.ds(video, 1), :], axis=1, keepdims=True) + 1


def note_kernel(device_ref, own_ref, other_ref, mate_dest_ref, mate_other_ref, *refs, steps):
    count = len(steps)
    query_refs, out_refs, home_ref = refs[: count - 1], refs[count - 1 : -1], refs[-1]
    first = query_refs[0].shape[0] - NOTE_ROWS
    device = device_ref[0]
    seat = lax.rem(device, 2 * count)
    front = device < 2 * count
    row = lax.broadcasted_iota(jnp.int32, (NOTE_ROWS, HD), 0)
    note = None
    for place, step in enumerate(steps):
        if note is None or own_ref.shape[0] > 1:
            video = (seat ^ step) // 2 * own_ref.shape[0] // count if own_ref.shape[0] > 1 else 0
            note = jnp.zeros((NOTE_ROWS, HD), jnp.int32)
            for line, (own, other) in enumerate(
                ((own_ref, other_ref), (mate_dest_ref, mate_other_ref))
            ):
                own, other = live_count(own, video), live_count(other, video)
                low, high = jnp.where(front, own, other), jnp.where(front, other, own)
                note = jnp.where(row == 2 * line, low, jnp.where(row == 2 * line + 1, high, note))
            note = note.astype(jnp.float32).astype(jnp.bfloat16)
        if place == 0:
            home_ref[...] = note
        else:
            out_refs[place - 1][first : first + NOTE_ROWS, :HD] = note


def attend_kernel(device_ref, guidance_ref, weight_ref, home_ref, *refs, score_scale, steps):
    count = len(steps)
    pack_refs, out_refs = refs[:-count], refs[-count:]
    own_refs, mate_refs = pack_refs[:count], pack_refs[count : 2 * count]
    query_refs = pack_refs[2 * count :]
    rows, per_pair = own_refs[0].shape[0] // 2, own_refs[0].shape[1]
    cap_half = rows // 2
    channels, width = weight_ref.shape
    device = device_ref[0]
    seat = lax.rem(device, 2 * count)
    start = seat // 2 * per_pair
    video = start // width
    scale = guidance_ref[video]
    front = device < 2 * count
    factor = jnp.where(front, scale, 1.0 - scale)
    weight = weight_ref[:, pl.ds(pl.multiple_of(lax.rem(start, width), HD), per_pair)]
    if out_refs[0].shape[1] > 1:
        for out_ref in out_refs:
            out_ref[...] = jnp.zeros_like(out_ref)

    slot = lax.broadcasted_iota(jnp.int32, (cap_half, HD), 0).astype(jnp.float32)
    masks = []
    for mate in range(2):
        for place in range(count):
            note = query_refs[place][FOLD * rows :, :HD] if place else home_ref[...]
            note = note.astype(jnp.float32)
            line = 2 * (mate if place == 0 else 1 - mate)
            for group in range(2):
                live = note[line + group : line + group + 1, :]
                masks.append(jnp.where(slot < live, 0.0, neg_big))
    mask = jnp.concatenate(masks)
    sources = (*own_refs, *mate_refs)
    block = max(1, HD // rows)
    for first in range(0, count, block):
        places = range(first, min(count, first + block))
        attended = []
        for column in range(0, per_pair, HD):
            span = slice(column, column + HD)
            fold, lane = divmod(column, per_pair // FOLD)
            query = jnp.concatenate(
                [
                    query_refs[place][fold * rows : (fold + 1) * rows, lane : lane + HD]
                    for place in places
                ]
            )
            key = jnp.concatenate([ref[:rows, span] for ref in sources])
            value = jnp.concatenate([ref[rows:, span] for ref in sources])
            scores = lax.dot_general(
                key, query, (((1,), (1,)), ((), ())), preferred_element_type=jnp.float32
            )
            scores = scores + mask[:, : query.shape[0]]
            top = jnp.max(scores, axis=0, keepdims=True)
            weights = jnp.exp2((scores - top) * (score_scale * math.log2(math.e)))
            share = 1.0 / jnp.sum(weights, axis=0, keepdims=True)
            probabilities = (weights * share).astype(jnp.bfloat16)
            attended.append(
                lax.dot_general(
                    value,
                    probabilities,
                    (((0,), (0,)), ((), ())),
                    preferred_element_type=jnp.float32,
                ).astype(jnp.bfloat16)
            )
        total = jnp.dot(
            weight, jnp.concatenate(attended, axis=0), preferred_element_type=jnp.float32
        )
        part = (total * factor).T.reshape(len(places), 2, 2, cap_half // 2, channels)
        part = jnp.concatenate([part[:, :, 0], part[:, :, 1]], axis=-1)
        for place in places:
            near, far = part[place - first, 0], part[place - first, 1]
            near, far = jnp.where(front, near, far), jnp.where(front, far, near)
            quad, line = steps[place] // 4, steps[place] // 2 % 2
            out_refs[quad][line, video] = near
            out_refs[count // 2 + quad][line, video] = far


def gather_kernel(*refs):
    *part_refs, kept_ref, sent_ref = refs
    for line, out_ref in enumerate((kept_ref, sent_ref)):
        terms = [ref[line] for ref in part_refs]
        while len(terms) > 1:
            terms = [sum(terms[i : i + 2]) for i in range(0, len(terms), 2)]
        out_ref[...] = terms[0]


def prepare_kernel(
    step_ref, dest_ref, latents_ref, spread_ref, means_ref, gains_ref, sigma_ref
):
    videos, tokens = dest_ref.shape
    channels = latents_ref.shape[2]
    cap_half = means_ref.shape[1]
    for video in range(videos):
        slot = lax.broadcasted_iota(jnp.int32, (cap_half, tokens), 0)
        onehot = (dest_ref[video : video + 1, :] == slot).astype(jnp.float32)
        tally = jnp.sum(onehot, axis=1, keepdims=True)
        count = jnp.maximum(tally, 1.0)
        latent_sums = jnp.dot(
            onehot,
            latents_ref[video],
            precision=lax.Precision.HIGHEST,
            preferred_element_type=jnp.float32,
        )
        step_value = jnp.full((1, channels), step_ref[video], jnp.int32).astype(jnp.float32)
        sigma_now = sigma_of(step_value)
        sigma_next = sigma_of(step_value + float(STRIDE))
        spread_ref[video] = jnp.concatenate([onehot] * 3, axis=0).T.astype(jnp.bfloat16)
        means_ref[video] = latent_sums / count
        gains_ref[video] = (sigma_next - sigma_now) * (tally / count)
        sigma_ref[video] = jnp.broadcast_to(sigma_now, sigma_ref.shape[1:])


def finish_kernel(
    kept_ref,
    came_ref,
    spread_ref,
    means_ref,
    gains_ref,
    sigma_ref,
    latents_ref,
    denoised_ref,
    merged_ref,
):
    videos, _, channels = latents_ref.shape
    for video in range(videos):
        lanes = kept_ref[video] + came_ref[video]
        merged = jnp.concatenate([lanes[:, :channels], lanes[:, channels:]], axis=0)
        merged_ref[video] = means_ref[video] + gains_ref[video] * merged
        top = merged.astype(jnp.bfloat16)
        rest = merged - top.astype(jnp.float32)
        middle = rest.astype(jnp.bfloat16)
        bottom = (rest - middle.astype(jnp.float32)).astype(jnp.bfloat16)
        velocity = jnp.dot(
            spread_ref[video],
            jnp.concatenate([top, middle, bottom], axis=0),
            preferred_element_type=jnp.float32,
        )
        denoised_ref[video] = latents_ref[video] - sigma_ref[video, :1] * velocity


def steps_of(half):
    first = [step for step in (0, 6, 2, 4) if step < half]
    return (*first, *range(8, half, 2))


def run(
    queries, keys, values, live_counts, merge_dest, latents, guidance, step_index, out_weight
):
    groups = lax.axis_size("seq")
    device = lax.axis_index("seq")
    half = groups // 2
    count = half // 2
    rows, columns = queries.shape
    videos = guidance.shape[0]
    _, channels = out_weight.shape
    per_pair = columns // count
    cap_half = rows // 2
    tokens = merge_dest.shape[1]
    smem = pl.BlockSpec(memory_space=pltpu.SMEM)
    vmem = pl.BlockSpec(memory_space=pltpu.VMEM)
    hbm = pl.BlockSpec(memory_space=pl.ANY)
    f32 = jnp.float32
    bf16 = queries.dtype

    def swap(part, step):
        return lax.ppermute(part, "seq", [(i, i ^ step) for i in range(groups)])

    steps = steps_of(half)
    seat = device.reshape(1)
    other_dest = swap(merge_dest, half)
    kv_shape = jax.ShapeDtypeStruct((2 * rows, per_pair), bf16)
    note_shape = jax.ShapeDtypeStruct((FOLD * rows + NOTE_ROWS, per_pair // FOLD), bf16)
    query_shape = jax.ShapeDtypeStruct((FOLD * rows, per_pair // FOLD), bf16)
    query_shapes = [query_shape] + [note_shape] * (count - 1)
    sources = [pltpu.with_memory_space_constraint(part, pltpu.HBM) for part in (queries, keys, values)]
    packed = pl.pallas_call(
        functools.partial(pack_kernel, steps=steps),
        out_shape=[kv_shape] * count + query_shapes,
        in_specs=[smem, hbm, hbm, hbm],
        out_specs=[vmem] * (2 * count),
        scratch_shapes=[pltpu.SemaphoreType.DMA((count * (2 + FOLD),))],
        compiler_params=small,
        name="pack",
    )(seat, *sources)
    own, asked = packed[:count], packed[count:]
    held = [own[0]] + [swap(own[place], steps[place]) for place in range(1, count)]
    mate_dest = swap(merge_dest, 1)
    mate_other = swap(other_dest, 1)
    *noted, home = pl.pallas_call(
        functools.partial(note_kernel, steps=steps),
        out_shape=[note_shape] * (count - 1) + [jax.ShapeDtypeStruct((NOTE_ROWS, HD), bf16)],
        in_specs=[smem] + [vmem] * (count + 3),
        out_specs=[vmem] * count,
        input_output_aliases={5 + place: place for place in range(count - 1)},
        compiler_params=small,
        name="note",
    )(
        seat,
        *(
            pltpu.with_memory_space_constraint(part, pltpu.VMEM)
            for part in (merge_dest, other_dest, mate_dest, mate_other)
        ),
        *asked[1:],
    )
    asked = [swap(part, steps[place] ^ 1) for place, part in enumerate((asked[0], *noted))]
    lent = [swap(held[0], 1)] + [swap(held[place], 1) for place in range(1, count)]
    part_shape = (videos, cap_half // 2, 2 * channels)
    parts = pl.pallas_call(
        functools.partial(attend_kernel, score_scale=1.0 / math.sqrt(HD), steps=steps),
        out_shape=[jax.ShapeDtypeStruct((2, *part_shape), f32)] * count,
        in_specs=[smem, smem] + [vmem] * (1 + 1 + 3 * count),
        out_specs=[vmem] * count,
        compiler_params=large,
        name="attend",
    )(seat, guidance, out_weight.T, home, *held, *lent, *asked)
    parts = [swap(parts[quad], 4 * quad + 1) for quad in range(count)]
    kept, sent = pl.pallas_call(
        gather_kernel,
        out_shape=[jax.ShapeDtypeStruct(part_shape, f32)] * 2,
        in_specs=[vmem] * count,
        out_specs=[vmem] * 2,
        compiler_params=small,
        name="gather",
    )(*parts)
    came = swap(sent, 2)
    prepared = pl.pallas_call(
        prepare_kernel,
        out_shape=(
            jax.ShapeDtypeStruct((videos, tokens, 3 * cap_half), jnp.bfloat16),
            jax.ShapeDtypeStruct((videos, cap_half, channels), f32),
            jax.ShapeDtypeStruct((videos, cap_half, channels), f32),
            jax.ShapeDtypeStruct((videos, 8, channels), f32),
        ),
        in_specs=[smem, vmem, vmem],
        out_specs=(vmem, vmem, vmem, vmem),
        compiler_params=small,
        name="prepare",
    )(step_index, merge_dest, latents)
    return pl.pallas_call(
        finish_kernel,
        out_shape=(
            jax.ShapeDtypeStruct((videos, tokens, channels), f32),
            jax.ShapeDtypeStruct((videos, cap_half, channels), f32),
        ),
        in_specs=[vmem] * 7,
        out_specs=(vmem, vmem),
        compiler_params=small,
        name="finish",
    )(kept, came, *prepared, latents)


def solution(mesh):
    placed = (
        P(("jobs", "seq"), None),
        P(("jobs", "seq"), None),
        P(("jobs", "seq"), None),
        P("jobs", "seq"),
        P("jobs", "seq"),
        P("jobs", "seq", None),
        P("jobs"),
        P("jobs"),
        P(),
    )
    return jax.shard_map(
        run,
        mesh=mesh,
        in_specs=placed,
        out_specs=(P("jobs", "seq", None), P("jobs", "seq", None)),
        check_vma=False,
    )
```

```python
import functools
import math

import jax
import jax.numpy as jnp
from jax import lax
from jax.experimental import pallas as pl
from jax.experimental.pallas import tpu as pltpu
from jax.sharding import PartitionSpec as P


HD = 128
NOTE_ROWS = 8
FOLD = 2
TIMESTEPS = 1000
STRIDE = 20

neg_big = -1e30
shift_value = 5.0
small = pltpu.CompilerParams(vmem_limit_bytes=16 * 2**20)
large = pltpu.CompilerParams(vmem_limit_bytes=32 * 2**20)


def sigma_of(step_value):
    frac = 1.0 - step_value / TIMESTEPS
    return shift_value * frac / (1.0 + (shift_value - 1.0) * frac)


def fetch(pieces, sems):
    copies = []
    for number, (source, target) in enumerate(pieces):
        copies.append(pltpu.make_async_copy(source, target, sems.at[number]))
        copies[-1].start()
    for copy in copies:
        copy.wait()


def pack_keys_kernel(device_ref, key_ref, value_ref, *refs, steps):
    *out_refs, sems = refs
    rows, columns = key_ref.shape
    per_pair = columns // len(steps)
    seat = lax.rem(device_ref[0], 2 * len(steps))
    pieces = []
    for place, step in enumerate(steps):
        span = pl.ds(pl.multiple_of((seat ^ step) // 2 * per_pair, HD), per_pair)
        pieces.append((key_ref.at[:, span], out_refs[place].at[pl.ds(0, rows), :]))
        pieces.append((value_ref.at[:, span], out_refs[place].at[pl.ds(rows, rows), :]))
    fetch(pieces, sems)


def pack_queries_kernel(device_ref, query_ref, *refs, steps):
    *out_refs, sems = refs
    rows, columns = query_ref.shape
    folded = columns // len(steps) // FOLD
    seat = lax.rem(device_ref[0], 2 * len(steps))
    pieces = []
    for place, step in enumerate(steps):
        for fold in range(FOLD):
            start = ((seat ^ step) // 2 * FOLD + fold) * folded
            span = pl.ds(pl.multiple_of(start, HD), folded)
            pieces.append((query_ref.at[:, span], out_refs[place].at[pl.ds(fold * rows, rows), :]))
    fetch(pieces, sems)


def live_count(dest_ref, video):
    return jnp.max(dest_ref[pl.ds(video, 1), :], axis=1, keepdims=True) + 1


def note_kernel(device_ref, own_ref, other_ref, mate_dest_ref, mate_other_ref, *refs, steps):
    count = len(steps)
    query_refs, out_refs, home_ref = refs[: count - 1], refs[count - 1 : -1], refs[-1]
    first = query_refs[0].shape[0] - NOTE_ROWS
    device = device_ref[0]
    seat = lax.rem(device, 2 * count)
    front = device < 2 * count
    row = lax.broadcasted_iota(jnp.int32, (NOTE_ROWS, HD), 0)
    note = None
    for place, step in enumerate(steps):
        if note is None or own_ref.shape[0] > 1:
            video = (seat ^ step) // 2 * own_ref.shape[0] // count if own_ref.shape[0] > 1 else 0
            note = jnp.zeros((NOTE_ROWS, HD), jnp.int32)
            for line, (own, other) in enumerate(
                ((own_ref, other_ref), (mate_dest_ref, mate_other_ref))
            ):
                own, other = live_count(own, video), live_count(other, video)
                low, high = jnp.where(front, own, other), jnp.where(front, other, own)
                note = jnp.where(row == 2 * line, low, jnp.where(row == 2 * line + 1, high, note))
            note = note.astype(jnp.float32).astype(jnp.bfloat16)
        if place == 0:
            home_ref[...] = note
        else:
            out_refs[place - 1][first : first + NOTE_ROWS, :HD] = note


def attend_kernel(device_ref, guidance_ref, weight_ref, home_ref, *refs, score_scale, steps):
    count = len(steps)
    pack_refs, out_refs = refs[:-count], refs[-count:]
    own_refs, mate_refs = pack_refs[:count], pack_refs[count : 2 * count]
    query_refs = pack_refs[2 * count :]
    rows, per_pair = own_refs[0].shape[0] // 2, own_refs[0].shape[1]
    cap_half = rows // 2
    channels, width = weight_ref.shape
    device = device_ref[0]
    seat = lax.rem(device, 2 * count)
    start = seat // 2 * per_pair
    video = start // width
    scale = guidance_ref[video]
    front = device < 2 * count
    factor = jnp.where(front, scale, 1.0 - scale)
    weight = weight_ref[:, pl.ds(pl.multiple_of(lax.rem(start, width), HD), per_pair)]
    if out_refs[0].shape[1] > 1:
        for out_ref in out_refs:
            out_ref[...] = jnp.zeros_like(out_ref)

    slot = lax.broadcasted_iota(jnp.int32, (cap_half, HD), 0).astype(jnp.float32)
    masks = []
    for mate in range(2):
        for place in range(count):
            note = query_refs[place][FOLD * rows :, :HD] if place else home_ref[...]
            note = note.astype(jnp.float32)
            line = 2 * (mate if place == 0 else 1 - mate)
            for group in range(2):
                live = note[line + group : line + group + 1, :]
                masks.append(jnp.where(slot < live, 0.0, neg_big))
    mask = jnp.concatenate(masks)
    sources = (*own_refs, *mate_refs)
    block = max(1, HD // rows)
    for first in range(0, count, block):
        places = range(first, min(count, first + block))
        attended = []
        for column in range(0, per_pair, HD):
            span = slice(column, column + HD)
            fold, lane = divmod(column, per_pair // FOLD)
            query = jnp.concatenate(
                [
                    query_refs[place][fold * rows : (fold + 1) * rows, lane : lane + HD]
                    for place in places
                ]
            )
            key = jnp.concatenate([ref[:rows, span] for ref in sources])
            value = jnp.concatenate([ref[rows:, span] for ref in sources])
            scores = lax.dot_general(
                key, query, (((1,), (1,)), ((), ())), preferred_element_type=jnp.float32
            )
            scores = scores * (score_scale * math.log2(math.e)) + mask[:, : query.shape[0]]
            top = jnp.max(scores, axis=0, keepdims=True)
            weights = jnp.exp2(scores - top)
            share = 1.0 / jnp.sum(weights, axis=0, keepdims=True)
            probabilities = (weights * share).astype(jnp.bfloat16)
            attended.append(
                lax.dot_general(
                    value,
                    probabilities,
                    (((0,), (0,)), ((), ())),
                    preferred_element_type=jnp.float32,
                ).astype(jnp.bfloat16)
            )
        total = jnp.dot(
            weight, jnp.concatenate(attended, axis=0), preferred_element_type=jnp.float32
        )
        part = (total * factor).T.reshape(len(places), 2, 2, cap_half // 2, channels)
        part = jnp.concatenate([part[:, :, 0], part[:, :, 1]], axis=-1)
        for place in places:
            near, far = part[place - first, 0], part[place - first, 1]
            near, far = jnp.where(front, near, far), jnp.where(front, far, near)
            quad, line = steps[place] // 4, steps[place] // 2 % 2
            out_refs[quad][line, video] = near
            out_refs[count // 2 + quad][line, video] = far


def gather_kernel(*refs):
    *part_refs, kept_ref, sent_ref = refs
    for line, out_ref in enumerate((kept_ref, sent_ref)):
        terms = [ref[line] for ref in part_refs]
        while len(terms) > 1:
            terms = [sum(terms[i : i + 2]) for i in range(0, len(terms), 2)]
        out_ref[...] = terms[0]


def prepare_kernel(
    step_ref, dest_ref, latents_ref, spread_ref, means_ref, gains_ref, sigma_ref
):
    videos, tokens = dest_ref.shape
    channels = latents_ref.shape[2]
    cap_half = means_ref.shape[1]
    for video in range(videos):
        slot = lax.broadcasted_iota(jnp.int32, (cap_half, tokens), 0)
        onehot = (dest_ref[video : video + 1, :] == slot).astype(jnp.float32)
        tally = jnp.sum(onehot, axis=1, keepdims=True)
        count = jnp.maximum(tally, 1.0)
        latent_sums = jnp.dot(
            onehot,
            latents_ref[video],
            precision=lax.Precision.HIGHEST,
            preferred_element_type=jnp.float32,
        )
        step_value = jnp.full((1, channels), step_ref[video], jnp.int32).astype(jnp.float32)
        sigma_now = sigma_of(step_value)
        sigma_next = sigma_of(step_value + float(STRIDE))
        spread_ref[video] = jnp.concatenate([onehot] * 3, axis=0).T.astype(jnp.bfloat16)
        means_ref[video] = latent_sums / count
        gains_ref[video] = (sigma_next - sigma_now) * (tally / count)
        sigma_ref[video] = jnp.broadcast_to(sigma_now, sigma_ref.shape[1:])


def finish_kernel(
    kept_ref,
    came_ref,
    spread_ref,
    means_ref,
    gains_ref,
    sigma_ref,
    latents_ref,
    denoised_ref,
    merged_ref,
):
    videos, _, channels = latents_ref.shape
    for video in range(videos):
        lanes = kept_ref[video] + came_ref[video]
        merged = jnp.concatenate([lanes[:, :channels], lanes[:, channels:]], axis=0)
        merged_ref[video] = means_ref[video] + gains_ref[video] * merged
        top = merged.astype(jnp.bfloat16)
        rest = merged - top.astype(jnp.float32)
        middle = rest.astype(jnp.bfloat16)
        bottom = (rest - middle.astype(jnp.float32)).astype(jnp.bfloat16)
        velocity = jnp.dot(
            spread_ref[video],
            jnp.concatenate([top, middle, bottom], axis=0),
            preferred_element_type=jnp.float32,
        )
        denoised_ref[video] = latents_ref[video] - sigma_ref[video, :1] * velocity


def steps_of(half):
    first = [step for step in (0, 6, 2, 4) if step < half]
    return (*first, *range(8, half, 2))


def run(
    queries, keys, values, live_counts, merge_dest, latents, guidance, step_index, out_weight
):
    groups = lax.axis_size("seq")
    device = lax.axis_index("seq")
    half = groups // 2
    count = half // 2
    rows, columns = queries.shape
    videos = guidance.shape[0]
    _, channels = out_weight.shape
    per_pair = columns // count
    cap_half = rows // 2
    tokens = merge_dest.shape[1]
    smem = pl.BlockSpec(memory_space=pltpu.SMEM)
    vmem = pl.BlockSpec(memory_space=pltpu.VMEM)
    hbm = pl.BlockSpec(memory_space=pl.ANY)
    f32 = jnp.float32
    bf16 = queries.dtype

    def swap(part, step):
        return lax.ppermute(part, "seq", [(i, i ^ step) for i in range(groups)])

    steps = steps_of(half)
    seat = device.reshape(1)
    other_dest = swap(merge_dest, half)
    kv_shape = jax.ShapeDtypeStruct((2 * rows, per_pair), bf16)
    note_shape = jax.ShapeDtypeStruct((FOLD * rows + NOTE_ROWS, per_pair // FOLD), bf16)
    query_shape = jax.ShapeDtypeStruct((FOLD * rows, per_pair // FOLD), bf16)
    query_shapes = [query_shape] + [note_shape] * (count - 1)
    sources = [pltpu.with_memory_space_constraint(part, pltpu.HBM) for part in (queries, keys, values)]
    own = pl.pallas_call(
        functools.partial(pack_keys_kernel, steps=steps),
        out_shape=[kv_shape] * count,
        in_specs=[smem, hbm, hbm],
        out_specs=[vmem] * count,
        scratch_shapes=[pltpu.SemaphoreType.DMA((2 * count,))],
        compiler_params=small,
        name="pack_keys",
    )(seat, *sources[1:])
    asked = pl.pallas_call(
        functools.partial(pack_queries_kernel, steps=steps),
        out_shape=query_shapes,
        in_specs=[smem, hbm],
        out_specs=[vmem] * count,
        scratch_shapes=[pltpu.SemaphoreType.DMA((FOLD * count,))],
        compiler_params=small,
        name="pack_queries",
    )(seat, sources[0])
    held = [own[0]] + [swap(own[place], steps[place]) for place in range(1, count)]
    mate_dest = swap(merge_dest, 1)
    mate_other = swap(other_dest, 1)
    *noted, home = pl.pallas_call(
        functools.partial(note_kernel, steps=steps),
        out_shape=[note_shape] * (count - 1) + [jax.ShapeDtypeStruct((NOTE_ROWS, HD), bf16)],
        in_specs=[smem] + [vmem] * (count + 3),
        out_specs=[vmem] * count,
        input_output_aliases={5 + place: place for place in range(count - 1)},
        compiler_params=small,
        name="note",
    )(
        seat,
        *(
            pltpu.with_memory_space_constraint(part, pltpu.VMEM)
            for part in (merge_dest, other_dest, mate_dest, mate_other)
        ),
        *asked[1:],
    )
    asked = [swap(part, steps[place] ^ 1) for place, part in enumerate((asked[0], *noted))]
    lent = [swap(held[0], 1)] + [swap(held[place], 1) for place in range(1, count)]
    part_shape = (videos, cap_half // 2, 2 * channels)
    parts = pl.pallas_call(
        functools.partial(attend_kernel, score_scale=1.0 / math.sqrt(HD), steps=steps),
        out_shape=[jax.ShapeDtypeStruct((2, *part_shape), f32)] * count,
        in_specs=[smem, smem] + [vmem] * (1 + 1 + 3 * count),
        out_specs=[vmem] * count,
        compiler_params=large,
        name="attend",
    )(seat, guidance, out_weight.T, home, *held, *lent, *asked)
    parts = [swap(parts[quad], 4 * quad + 1) for quad in range(count)]
    kept, sent = pl.pallas_call(
        gather_kernel,
        out_shape=[jax.ShapeDtypeStruct(part_shape, f32)] * 2,
        in_specs=[vmem] * count,
        out_specs=[vmem] * 2,
        compiler_params=small,
        name="gather",
    )(*parts)
    came = swap(sent, 2)
    prepared = pl.pallas_call(
        prepare_kernel,
        out_shape=(
            jax.ShapeDtypeStruct((videos, tokens, 3 * cap_half), jnp.bfloat16),
            jax.ShapeDtypeStruct((videos, cap_half, channels), f32),
            jax.ShapeDtypeStruct((videos, cap_half, channels), f32),
            jax.ShapeDtypeStruct((videos, 8, channels), f32),
        ),
        in_specs=[smem, vmem, vmem],
        out_specs=(vmem, vmem, vmem, vmem),
        compiler_params=small,
        name="prepare",
    )(step_index, merge_dest, latents)
    return pl.pallas_call(
        finish_kernel,
        out_shape=(
            jax.ShapeDtypeStruct((videos, tokens, channels), f32),
            jax.ShapeDtypeStruct((videos, cap_half, channels), f32),
        ),
        in_specs=[vmem] * 7,
        out_specs=(vmem, vmem),
        compiler_params=small,
        name="finish",
    )(kept, came, *prepared, latents)


def solution(mesh):
    placed = (
        P(("jobs", "seq"), None),
        P(("jobs", "seq"), None),
        P(("jobs", "seq"), None),
        P("jobs", "seq"),
        P("jobs", "seq"),
        P("jobs", "seq", None),
        P("jobs"),
        P("jobs"),
        P(),
    )
    return jax.shard_map(
        run,
        mesh=mesh,
        in_specs=placed,
        out_specs=(P("jobs", "seq", None), P("jobs", "seq", None)),
        check_vma=False,
    )
```

```python
import functools
import math

import jax
import jax.numpy as jnp
from jax import lax
from jax.experimental import pallas as pl
from jax.experimental.pallas import tpu as pltpu
from jax.sharding import PartitionSpec as P


HD = 128
NOTE_ROWS = 8
FOLD = 2
TIMESTEPS = 1000
STRIDE = 20

neg_big = -1e30
shift_value = 5.0
small = pltpu.CompilerParams(vmem_limit_bytes=16 * 2**20)
large = pltpu.CompilerParams(vmem_limit_bytes=32 * 2**20)


def sigma_of(step_value):
    frac = 1.0 - step_value / TIMESTEPS
    return shift_value * frac / (1.0 + (shift_value - 1.0) * frac)


def fetch(pieces, sems):
    copies = []
    for number, (source, target) in enumerate(pieces):
        copies.append(pltpu.make_async_copy(source, target, sems.at[number]))
        copies[-1].start()
    for copy in copies:
        copy.wait()


def pack_keys_kernel(device_ref, key_ref, value_ref, *refs, steps):
    *out_refs, sems = refs
    rows, columns = key_ref.shape
    per_pair = columns // len(steps)
    seat = lax.rem(device_ref[0], 2 * len(steps))
    pieces = []
    for place, step in enumerate(steps):
        span = pl.ds(pl.multiple_of((seat ^ step) // 2 * per_pair, HD), per_pair)
        pieces.append((key_ref.at[:, span], out_refs[place].at[pl.ds(0, rows), :]))
        pieces.append((value_ref.at[:, span], out_refs[place].at[pl.ds(rows, rows), :]))
    fetch(pieces, sems)


def pack_queries_kernel(device_ref, query_ref, *refs, steps):
    *out_refs, sems = refs
    rows, columns = query_ref.shape
    folded = columns // len(steps) // FOLD
    seat = lax.rem(device_ref[0], 2 * len(steps))
    pieces = []
    for place, step in enumerate(steps):
        for fold in range(FOLD):
            start = ((seat ^ step) // 2 * FOLD + fold) * folded
            span = pl.ds(pl.multiple_of(start, HD), folded)
            pieces.append((query_ref.at[:, span], out_refs[place].at[pl.ds(fold * rows, rows), :]))
    fetch(pieces, sems)


def live_count(dest_ref, video):
    return jnp.max(dest_ref[pl.ds(video, 1), :], axis=1, keepdims=True) + 1


def note_kernel(device_ref, own_ref, other_ref, mate_dest_ref, mate_other_ref, *refs, steps):
    count = len(steps)
    query_refs, out_refs, home_ref = refs[: count - 1], refs[count - 1 : -1], refs[-1]
    first = query_refs[0].shape[0] - NOTE_ROWS
    device = device_ref[0]
    seat = lax.rem(device, 2 * count)
    front = device < 2 * count
    row = lax.broadcasted_iota(jnp.int32, (NOTE_ROWS, HD), 0)
    note = None
    for place, step in enumerate(steps):
        if note is None or own_ref.shape[0] > 1:
            video = (seat ^ step) // 2 * own_ref.shape[0] // count if own_ref.shape[0] > 1 else 0
            note = jnp.zeros((NOTE_ROWS, HD), jnp.int32)
            for line, (own, other) in enumerate(
                ((own_ref, other_ref), (mate_dest_ref, mate_other_ref))
            ):
                own, other = live_count(own, video), live_count(other, video)
                low, high = jnp.where(front, own, other), jnp.where(front, other, own)
                note = jnp.where(row == 2 * line, low, jnp.where(row == 2 * line + 1, high, note))
            note = note.astype(jnp.float32).astype(jnp.bfloat16)
        if place == 0:
            home_ref[...] = note
        else:
            out_refs[place - 1][first : first + NOTE_ROWS, :HD] = note


def attend_kernel(device_ref, guidance_ref, weight_ref, home_ref, *refs, score_scale, steps):
    count = len(steps)
    pack_refs, out_refs = refs[:-2], refs[-2:]
    own_refs, mate_refs = pack_refs[:count], pack_refs[count : 2 * count]
    query_refs = pack_refs[2 * count :]
    rows, per_pair = own_refs[0].shape[0] // 2, own_refs[0].shape[1]
    cap_half = rows // 2
    channels, width = weight_ref.shape
    device = device_ref[0]
    seat = lax.rem(device, 2 * count)
    start = seat // 2 * per_pair
    video = start // width
    scale = guidance_ref[video]
    front = device < 2 * count
    factor = jnp.where(front, scale, 1.0 - scale)
    weight = weight_ref[:, pl.ds(pl.multiple_of(lax.rem(start, width), HD), per_pair)]
    if out_refs[0].shape[1] > 1:
        for out_ref in out_refs:
            out_ref[...] = jnp.zeros_like(out_ref)

    slot = lax.broadcasted_iota(jnp.int32, (cap_half, HD), 0).astype(jnp.float32)
    masks = []
    for mate in range(2):
        for place in range(count):
            note = query_refs[place][FOLD * rows :, :HD] if place else home_ref[...]
            note = note.astype(jnp.float32)
            line = 2 * (mate if place == 0 else 1 - mate)
            for group in range(2):
                live = note[line + group : line + group + 1, :]
                masks.append(jnp.where(slot < live, 0.0, neg_big))
    mask = jnp.concatenate(masks)
    sources = (*own_refs, *mate_refs)
    block = max(1, HD // rows)
    for first in range(0, count, block):
        places = range(first, min(count, first + block))
        attended = []
        for column in range(0, per_pair, HD):
            span = slice(column, column + HD)
            fold, lane = divmod(column, per_pair // FOLD)
            query = jnp.concatenate(
                [
                    query_refs[place][fold * rows : (fold + 1) * rows, lane : lane + HD]
                    for place in places
                ]
            )
            key = jnp.concatenate([ref[:rows, span] for ref in sources])
            value = jnp.concatenate([ref[rows:, span] for ref in sources])
            scores = lax.dot_general(
                key, query, (((1,), (1,)), ((), ())), preferred_element_type=jnp.float32
            )
            scores = scores * (score_scale * math.log2(math.e)) + mask[:, : query.shape[0]]
            top = jnp.max(scores, axis=0, keepdims=True)
            weights = jnp.exp2(scores - top)
            share = 1.0 / jnp.sum(weights, axis=0, keepdims=True)
            probabilities = (weights * share).astype(jnp.bfloat16)
            attended.append(
                lax.dot_general(
                    value,
                    probabilities,
                    (((0,), (0,)), ((), ())),
                    preferred_element_type=jnp.float32,
                ).astype(jnp.bfloat16)
            )
        total = jnp.dot(
            weight, jnp.concatenate(attended, axis=0), preferred_element_type=jnp.float32
        )
        part = (total * factor).T.reshape(len(places), 2, 2, cap_half // 2, channels)
        part = jnp.concatenate([part[:, :, 0], part[:, :, 1]], axis=-1)
        for place in places:
            near, far = part[place - first, 0], part[place - first, 1]
            near, far = jnp.where(front, near, far), jnp.where(front, far, near)
            quad, line = steps[place] // 4, steps[place] // 2 % 2
            out_refs[line][quad, video] = near
            out_refs[line][count // 2 + quad, video] = far


def add_lines_kernel(kept_ref, came_ref, *out_refs):
    for quad, out_ref in enumerate(out_refs):
        out_ref[...] = kept_ref[quad] + came_ref[quad]


def prepare_kernel(
    step_ref, dest_ref, latents_ref, spread_ref, means_ref, gains_ref, sigma_ref
):
    videos, tokens = dest_ref.shape
    channels = latents_ref.shape[2]
    cap_half = means_ref.shape[1]
    for video in range(videos):
        slot = lax.broadcasted_iota(jnp.int32, (cap_half, tokens), 0)
        onehot = (dest_ref[video : video + 1, :] == slot).astype(jnp.float32)
        tally = jnp.sum(onehot, axis=1, keepdims=True)
        count = jnp.maximum(tally, 1.0)
        latent_sums = jnp.dot(
            onehot,
            latents_ref[video],
            precision=lax.Precision.HIGHEST,
            preferred_element_type=jnp.float32,
        )
        step_value = jnp.full((1, channels), step_ref[video], jnp.int32).astype(jnp.float32)
        sigma_now = sigma_of(step_value)
        sigma_next = sigma_of(step_value + float(STRIDE))
        spread_ref[video] = jnp.concatenate([onehot] * 3, axis=0).T.astype(jnp.bfloat16)
        means_ref[video] = latent_sums / count
        gains_ref[video] = (sigma_next - sigma_now) * (tally / count)
        sigma_ref[video] = jnp.broadcast_to(sigma_now, sigma_ref.shape[1:])


def finish_kernel(*refs):
    spread_ref, means_ref, gains_ref, sigma_ref, latents_ref, denoised_ref, merged_ref = refs[-7:]
    videos, _, channels = latents_ref.shape
    for video in range(videos):
        terms = [ref[video] for ref in refs[:-7]]
        while len(terms) > 1:
            terms = [sum(terms[i : i + 2]) for i in range(0, len(terms), 2)]
        lanes = terms[0]
        merged = jnp.concatenate([lanes[:, :channels], lanes[:, channels:]], axis=0)
        merged_ref[video] = means_ref[video] + gains_ref[video] * merged
        top = merged.astype(jnp.bfloat16)
        rest = merged - top.astype(jnp.float32)
        middle = rest.astype(jnp.bfloat16)
        bottom = (rest - middle.astype(jnp.float32)).astype(jnp.bfloat16)
        velocity = jnp.dot(
            spread_ref[video],
            jnp.concatenate([top, middle, bottom], axis=0),
            preferred_element_type=jnp.float32,
        )
        denoised_ref[video] = latents_ref[video] - sigma_ref[video, :1] * velocity


def steps_of(half):
    first = [step for step in (0, 6, 2, 4) if step < half]
    return (*first, *range(8, half, 2))


def run(
    queries, keys, values, live_counts, merge_dest, latents, guidance, step_index, out_weight
):
    groups = lax.axis_size("seq")
    device = lax.axis_index("seq")
    half = groups // 2
    count = half // 2
    rows, columns = queries.shape
    videos = guidance.shape[0]
    _, channels = out_weight.shape
    per_pair = columns // count
    cap_half = rows // 2
    tokens = merge_dest.shape[1]
    smem = pl.BlockSpec(memory_space=pltpu.SMEM)
    vmem = pl.BlockSpec(memory_space=pltpu.VMEM)
    hbm = pl.BlockSpec(memory_space=pl.ANY)
    f32 = jnp.float32
    bf16 = queries.dtype

    def swap(part, step):
        return lax.ppermute(part, "seq", [(i, i ^ step) for i in range(groups)])

    steps = steps_of(half)
    seat = device.reshape(1)
    other_dest = swap(merge_dest, half)
    kv_shape = jax.ShapeDtypeStruct((2 * rows, per_pair), bf16)
    note_shape = jax.ShapeDtypeStruct((FOLD * rows + NOTE_ROWS, per_pair // FOLD), bf16)
    query_shape = jax.ShapeDtypeStruct((FOLD * rows, per_pair // FOLD), bf16)
    query_shapes = [query_shape] + [note_shape] * (count - 1)
    sources = [pltpu.with_memory_space_constraint(part, pltpu.HBM) for part in (queries, keys, values)]
    own = pl.pallas_call(
        functools.partial(pack_keys_kernel, steps=steps),
        out_shape=[kv_shape] * count,
        in_specs=[smem, hbm, hbm],
        out_specs=[vmem] * count,
        scratch_shapes=[pltpu.SemaphoreType.DMA((2 * count,))],
        compiler_params=small,
        name="pack_keys",
    )(seat, *sources[1:])
    asked = pl.pallas_call(
        functools.partial(pack_queries_kernel, steps=steps),
        out_shape=query_shapes,
        in_specs=[smem, hbm],
        out_specs=[vmem] * count,
        scratch_shapes=[pltpu.SemaphoreType.DMA((FOLD * count,))],
        compiler_params=small,
        name="pack_queries",
    )(seat, sources[0])
    held = [own[0]] + [swap(own[place], steps[place]) for place in range(1, count)]
    mate_dest = swap(merge_dest, 1)
    mate_other = swap(other_dest, 1)
    *noted, home = pl.pallas_call(
        functools.partial(note_kernel, steps=steps),
        out_shape=[note_shape] * (count - 1) + [jax.ShapeDtypeStruct((NOTE_ROWS, HD), bf16)],
        in_specs=[smem] + [vmem] * (count + 3),
        out_specs=[vmem] * count,
        input_output_aliases={5 + place: place for place in range(count - 1)},
        compiler_params=small,
        name="note",
    )(
        seat,
        *(
            pltpu.with_memory_space_constraint(part, pltpu.VMEM)
            for part in (merge_dest, other_dest, mate_dest, mate_other)
        ),
        *asked[1:],
    )
    asked = [swap(part, steps[place] ^ 1) for place, part in enumerate((asked[0], *noted))]
    lent = [swap(held[0], 1)] + [swap(held[place], 1) for place in range(1, count)]
    part_shape = (videos, cap_half // 2, 2 * channels)
    kept, sent = pl.pallas_call(
        functools.partial(attend_kernel, score_scale=1.0 / math.sqrt(HD), steps=steps),
        out_shape=[jax.ShapeDtypeStruct((count, *part_shape), f32)] * 2,
        in_specs=[smem, smem] + [vmem] * (1 + 1 + 3 * count),
        out_specs=[vmem] * 2,
        compiler_params=large,
        name="attend",
    )(seat, guidance, out_weight.T, home, *held, *lent, *asked)
    came = swap(sent, 2)
    parts = pl.pallas_call(
        add_lines_kernel,
        out_shape=[jax.ShapeDtypeStruct(part_shape, f32)] * count,
        in_specs=[vmem] * 2,
        out_specs=[vmem] * count,
        compiler_params=small,
        name="add_lines",
    )(kept, came)
    parts = [swap(parts[quad], 4 * quad + 1) for quad in range(count)]
    prepared = pl.pallas_call(
        prepare_kernel,
        out_shape=(
            jax.ShapeDtypeStruct((videos, tokens, 3 * cap_half), jnp.bfloat16),
            jax.ShapeDtypeStruct((videos, cap_half, channels), f32),
            jax.ShapeDtypeStruct((videos, cap_half, channels), f32),
            jax.ShapeDtypeStruct((videos, 8, channels), f32),
        ),
        in_specs=[smem, vmem, vmem],
        out_specs=(vmem, vmem, vmem, vmem),
        compiler_params=small,
        name="prepare",
    )(step_index, merge_dest, latents)
    return pl.pallas_call(
        finish_kernel,
        out_shape=(
            jax.ShapeDtypeStruct((videos, tokens, channels), f32),
            jax.ShapeDtypeStruct((videos, cap_half, channels), f32),
        ),
        in_specs=[vmem] * (count + 5),
        out_specs=(vmem, vmem),
        compiler_params=small,
        name="finish",
    )(*parts, *prepared, latents)


def solution(mesh):
    placed = (
        P(("jobs", "seq"), None),
        P(("jobs", "seq"), None),
        P(("jobs", "seq"), None),
        P("jobs", "seq"),
        P("jobs", "seq"),
        P("jobs", "seq", None),
        P("jobs"),
        P("jobs"),
        P(),
    )
    return jax.shard_map(
        run,
        mesh=mesh,
        in_specs=placed,
        out_specs=(P("jobs", "seq", None), P("jobs", "seq", None)),
        check_vma=False,
    )
```
